512 devices in a mesh: grp: 8 (over x, core), own: 64 (over z, y).
Axes of the slice: x: 4, y: 4, z: 16, core: 2. Of those that a mesh axis runs over, the one named last changes fastest.
Arguments:
- left: bfloat16 [32768, 128, 64], P(('grp', 'own')), may hold values from -0.75 to 0.75
- right: bfloat16 [32768, 128, 64], P(('grp', 'own')), may hold values from -0.75 to 0.75
- values: bfloat16 [32768, 128], P(('grp', 'own')), may hold values from -6 to 6
- core: bfloat16 [10240, 64, 64], P(('grp', 'own')), may hold values from -6 to 6
- tile_slice: int32 [32768], P(('grp', 'own')), may hold values from 0 to 10239, as said below
- tile_fill: int32 [32768], P(('grp', 'own')), may hold values from 64 to 128
Outputs:
- new_core: bfloat16 [10240, 64, 64], P(('grp', 'own'))
- new_left: bfloat16 [32768, 128, 64], P(('grp', 'own'))
The draws below stay inside these ranges and needn't reach their ends.
Inputs may be any that keep to these rules, and one draw needn't show every extreme that they name: `tile_slice`: call j // 20 the block of slice j and its remainder mod 64 its class. Among the tiles of one device at most 2 have slices of one class; in every group of 64 consecutive devices some class gets exactly 2 tiles from every device of the group.
All inputs are finite; a program needn't handle non-finite values.
Results may differ from the reference program's by a relative error of at most 0.0052.
Values may be sent and summed in bfloat16 or wider, within the bound.
No kernel may reach another device: no remote copies, remote signals or barrier semaphores. Data moves between devices by JAX's collectives and lax.ppermute only.
A program may use at most 64 MiB of HBM per device.

```python
import jax
import jax.numpy as jnp
from jax import lax

RANK = 64
TILE = 128
SLICES = 10240
TILES_DEV = 64
TILES = 32768
OWNERS = 64
GROUPS = 8
SL_DEV = 20


def draw_tile_slice(key, part):
    dev_total = TILES // TILES_DEV
    fill_base = TILES_DEV // OWNERS
    slot_cap = 2 * fill_base
    pair_count = OWNERS // 2

    def one_device(device):
        key_block = jax.random.fold_in(key, device)
        key_group = jax.random.fold_in(jax.random.fold_in(key, 7919), device // OWNERS)
        shifts = jax.random.randint(jax.random.fold_in(key_block, 1), (pair_count,), -fill_base, fill_base + 1)
        chosen = jax.random.randint(key_group, (), 0, pair_count)
        sign_value = 2 * jax.random.randint(jax.random.fold_in(key_group, 1), (), 0, 2) - 1
        shifts = jnp.where(jnp.arange(pair_count) == chosen, sign_value * fill_base, shifts)
        counts = jnp.stack([fill_base + shifts, fill_base - shifts], axis=1).reshape(-1)
        slot_owner = jnp.repeat(jnp.arange(OWNERS), slot_cap)
        slot_rank = jnp.tile(jnp.arange(slot_cap), OWNERS)
        live_slots = slot_rank < counts[slot_owner]
        slot_order = jnp.argsort(jnp.where(live_slots, 0, 1), stable=True)
        chosen_owner = slot_owner[slot_order[:TILES_DEV]]
        chosen_owner = jax.random.permutation(jax.random.fold_in(key_block, 2), chosen_owner)
        group_pick = jax.random.randint(jax.random.fold_in(key_block, 3), (TILES_DEV,), 0, GROUPS)
        offsets = jax.random.randint(jax.random.fold_in(key_block, 4), (TILES_DEV,), 0, SL_DEV)
        return ((group_pick * OWNERS + chosen_owner) * SL_DEV + offsets).astype(jnp.int32)
    return jax.vmap(one_device)(jnp.arange(dev_total)).reshape(-1)


def place_ends(values, stream_key, smallest, high):
    longest = values.shape.index(max(values.shape))
    spots = []
    for shift in (0, 1):
        where = [jax.random.randint(jax.random.fold_in(stream_key, axis), (), 0, length) for axis, length in enumerate(values.shape)]
        where[longest] = (where[longest] + shift) % values.shape[longest]
        spots.append(tuple(where))
    return values.at[spots[0]].set(smallest).at[spots[1]].set(high)


def level_of(key, extent, split, smallest, top_value):
    loudness, own = 1.0, jax.random.fold_in(key, 6)
    for position, parts in split:
        steps = jnp.exp(jax.random.uniform(jax.random.fold_in(own, position), (parts,), jnp.float32, smallest / len(split), top_value / len(split)))
        loudness = loudness * jnp.repeat(steps, extent[position] // parts).reshape([-1 if axis == position else 1 for axis in range(len(extent))])
    return loudness


def normal_values(stream_key, shape, spread, reach, shards=(), kind=jnp.bfloat16):
    gain = level_of(stream_key, shape, shards, -0.22, 0.18) if shards else 1.0
    entries = jax.random.normal(stream_key, shape, jnp.float32) * spread * gain
    return jnp.minimum(jnp.maximum(entries, -reach), reach).astype(kind)


def setup_inputs(seed: int = 0) -> dict:
    keys = jax.random.split(jax.random.key(seed), 7)
    left = normal_values(keys[0], (TILES, TILE, RANK), 0.125, 0.75, ((0, 512),))
    right = normal_values(keys[1], (TILES, TILE, RANK), 0.125, 0.75, ((0, 512),))
    values = normal_values(keys[2], (TILES, TILE), 1.0, 6.0, ((0, 512),))
    core = normal_values(keys[3], (SLICES, RANK, RANK), 1.0, 6.0, ((0, 512),))
    tile_slice = draw_tile_slice(jax.random.fold_in(keys[6], 71), 0)
    tile_fill = place_ends(jax.random.randint(keys[5], (TILES,), TILE // 2, TILE + 1), jax.random.fold_in(keys[5], 1), TILE // 2, TILE).astype(jnp.int32)
    return dict(left=left, right=right, values=values, core=core, tile_slice=tile_slice, tile_fill=tile_fill)


def tile_gradients(packed):
    left_tiles, right_tiles, value_tiles, slice_ids, fill_counts, core_table = packed
    slice_tables = core_table[slice_ids].astype(jnp.float32)
    projected = jnp.einsum('sea,sab->seb', left_tiles.astype(jnp.float32), slice_tables, precision=lax.Precision.HIGHEST)
    predicted = jnp.sum(projected * right_tiles.astype(jnp.float32), axis=-1)
    live_rows = jnp.arange(TILE)[None, :] < fill_counts[:, None]
    residual = jnp.where(live_rows, predicted - value_tiles.astype(jnp.float32), jnp.float32(0.0))
    weighted = (residual[:, :, None] * left_tiles.astype(jnp.float32)).astype(jnp.bfloat16)
    return jnp.einsum('sea,seb->sab', weighted.astype(jnp.float32), right_tiles.astype(jnp.float32), precision=lax.Precision.HIGHEST)


def reference(left, right, values, core, tile_slice, tile_fill):
    block_count = TILES // TILES_DEV
    left_blocks = left.reshape(block_count, TILES_DEV, TILE, RANK)
    right_blocks = right.reshape(block_count, TILES_DEV, TILE, RANK)
    value_blocks = values.reshape(block_count, TILES_DEV, TILE)
    slice_blocks = tile_slice.reshape(block_count, TILES_DEV)
    fill_blocks = tile_fill.reshape(block_count, TILES_DEV)

    def grads_of(index):
        return tile_gradients((left_blocks[index], right_blocks[index], value_blocks[index], slice_blocks[index], fill_blocks[index], core))

    tile_grads = lax.map(grads_of, jnp.arange(block_count)).reshape(TILES, RANK, RANK)
    gradient = jax.ops.segment_sum(tile_grads, tile_slice, num_segments=SLICES)
    new_core = (core.astype(jnp.float32) - gradient).astype(jnp.bfloat16)

    def refresh_of(index):
        slice_tables = new_core[slice_blocks[index]].astype(jnp.float32)
        refreshed = jnp.einsum('sea,sab->seb', left_blocks[index].astype(jnp.float32), slice_tables, precision=lax.Precision.HIGHEST)
        return refreshed.astype(jnp.bfloat16)

    new_left = lax.map(refresh_of, jnp.arange(block_count)).reshape(TILES, TILE, RANK)
    return new_core, new_left
```

```python
import functools

import jax
import jax.numpy as jnp
from jax import lax
from jax.experimental import pallas as pl
from jax.experimental.pallas import tpu as pltpu
from jax.sharding import PartitionSpec as P

VMEM = pl.BlockSpec(memory_space=pltpu.VMEM)
SMEM = pl.BlockSpec(memory_space=pltpu.SMEM)
BF16 = jnp.bfloat16
F32 = jnp.float32


def pack(square):
    half = square.shape[0] // 2
    return jnp.concatenate([square[:half], square[half:]], axis=1)


def unpack(packed):
    width = packed.shape[1] // 2
    return jnp.concatenate([packed[:, :width], packed[:, width:]], axis=0)


def pack_kernel(core_ref, out_ref):
    for i in range(core_ref.shape[0]):
        out_ref[i] = pack(core_ref[i].astype(F32).T).astype(BF16)


def pick_kernel(ids_ref, table_ref, out_ref):
    def step(k, carry):
        out_ref[k] = table_ref[jnp.maximum(ids_ref[k], 0)]
        return carry

    lax.fori_loop(0, out_ref.shape[0], step, 0, unroll=8)


def grad_kernel(slot_ref, fill_ref, left_ref, right_ref, value_ref, slice_ref, out_ref, value_scr):
    value_scr[...] = value_ref[...].astype(F32)
    lanes = lax.broadcasted_iota(jnp.int32, (1, left_ref.shape[2]), 1)

    def step(t, carry):
        slot = slot_ref[t]
        left = left_ref[t]
        right = right_ref[t]
        table = unpack(slice_ref[slot])
        projected = jnp.dot(table, left, preferred_element_type=F32)
        predicted = jnp.sum(projected * right.astype(F32), axis=0, keepdims=True)
        residual = jnp.where(lanes < fill_ref[t], predicted - value_scr[pl.ds(t, 1), :], 0.0)
        weighted = (residual * left.astype(F32)).astype(BF16)
        grad = lax.dot_general(
            right, weighted, (((1,), (1,)), ((), ())), preferred_element_type=F32
        )
        out_ref[slot] = pack(grad).astype(BF16)
        return carry

    lax.fori_loop(0, left_ref.shape[0], step, 0, unroll=8)


def sum_kernel(ids_ref, grad_ref, out_ref, acc_ref):
    acc_ref[...] = jnp.zeros_like(acc_ref)

    def step(k, carry):
        @pl.when(ids_ref[k] >= 0)
        def _():
            acc_ref[ids_ref[k]] += grad_ref[k].astype(F32)

        return carry

    lax.fori_loop(0, grad_ref.shape[0], step, 0, unroll=4)
    out_ref[...] = acc_ref[...].astype(BF16)


def update_kernel(table_ref, part_ref, packed_ref, out_ref):
    total = jnp.sum(part_ref[...].astype(F32), axis=0)
    packed_ref[...] = (table_ref[...].astype(F32) - total).astype(BF16)
    for i in range(out_ref.shape[0]):
        out_ref[i] = unpack(packed_ref[i].astype(F32)).T.astype(BF16)


def refresh_kernel(slot_ref, left_ref, slice_ref, out_ref):
    def step(t, carry):
        table = unpack(slice_ref[slot_ref[t]])
        out_ref[t] = jnp.dot(table, left_ref[t], preferred_element_type=F32).astype(BF16)
        return carry

    lax.fori_loop(0, left_ref.shape[0], step, 0, unroll=8)


def call(kernel, in_specs, outs, scratch=(), flops=10**6, moved=4 * 10**6):
    many = isinstance(outs, tuple)
    return pl.pallas_call(
        kernel,
        out_shape=outs,
        in_specs=in_specs,
        out_specs=(VMEM,) * len(outs) if many else VMEM,
        scratch_shapes=list(scratch),
        cost_estimate=pl.CostEstimate(flops=flops, bytes_accessed=moved, transcendentals=0),
    )


def exchange(x, axis):
    return lax.all_to_all(x, axis, split_axis=0, concat_axis=0, tiled=True)


def body(left, right, values, core, tile_slice, tile_fill):
    owners = lax.axis_size("own")
    groups = lax.axis_size("grp")
    tiles, rows, rank = left.shape
    per_device = core.shape[0]
    local_count = groups * per_device
    slots = 2 * owners
    packed_shape = (rank // 2, 2 * rank)

    block = tile_slice // per_device
    owner = block % owners
    local = block // owners * per_device + tile_slice % per_device
    position = jnp.arange(tiles)
    same = (owner[:, None] == owner[None, :]) & (position[None, :] < position[:, None])
    slot = 2 * owner + jnp.sum(same.astype(jnp.int32), axis=1)
    hit = slot[None, :] == jnp.arange(slots)[:, None]
    wanted = jnp.max(jnp.where(hit, local[None, :], -1), axis=1)

    left_t = jnp.swapaxes(left, 1, 2)
    right_t = jnp.swapaxes(right, 1, 2)
    sds = jax.ShapeDtypeStruct
    slot_sds = sds((slots,) + packed_shape, BF16)

    mine = call(pack_kernel, [VMEM], sds((per_device,) + packed_shape, BF16))(core)
    ids = exchange(wanted.reshape(owners, 2), "own").reshape(slots)
    spread = jnp.broadcast_to(mine[None], (groups,) + mine.shape).reshape((local_count,) + packed_shape)
    tables = exchange(spread, "grp")
    outgoing = call(pick_kernel, [SMEM, VMEM], slot_sds)(ids, tables)
    got = exchange(outgoing, "own")
    grads = call(
        grad_kernel,
        [SMEM, SMEM, VMEM, VMEM, VMEM, VMEM],
        slot_sds,
        [pltpu.VMEM((tiles, rows), F32)],
    )(slot, tile_fill, left_t, right_t, values, got)
    got_grads = exchange(grads, "own")
    partial = call(
        sum_kernel,
        [SMEM, VMEM],
        sds((local_count,) + packed_shape, BF16),
        [pltpu.VMEM((local_count,) + packed_shape, F32)],
    )(ids, got_grads)
    parts = exchange(partial, "grp").reshape((groups, per_device) + packed_shape)
    new_mine, new_core = call(
        update_kernel,
        [VMEM, VMEM],
        (sds((per_device,) + packed_shape, BF16), sds(core.shape, BF16)),
    )(mine, parts)
    new_spread = jnp.broadcast_to(new_mine[None], (groups,) + mine.shape).reshape(spread.shape)
    new_tables = exchange(new_spread, "grp")
    new_outgoing = call(pick_kernel, [SMEM, VMEM], slot_sds)(ids, new_tables)
    new_got = exchange(new_outgoing, "own")
    new_left_t = call(refresh_kernel, [SMEM, VMEM, VMEM], sds(left_t.shape, BF16))(
        slot, left_t, new_got
    )
    return (new_core, jnp.swapaxes(new_left_t, 1, 2))


def solution(mesh):
    spec3 = P(("grp", "own"), None, None)
    spec2 = P(("grp", "own"), None)
    spec1 = P(("grp", "own"))
    return jax.shard_map(
        body,
        mesh=mesh,
        in_specs=(spec3, spec3, spec2, spec3, spec1, spec1),
        out_specs=(spec3, spec3),
        check_vma=False,
    )
```

```python
import functools

import jax
import jax.numpy as jnp
from jax import lax
from jax.experimental import pallas as pl
from jax.experimental.pallas import tpu as pltpu
from jax.sharding import PartitionSpec as P

VMEM = pl.BlockSpec(memory_space=pltpu.VMEM)
SMEM = pl.BlockSpec(memory_space=pltpu.SMEM)
BF16 = jnp.bfloat16
F32 = jnp.float32


def pack(square):
    half = square.shape[0] // 2
    return jnp.concatenate([square[:half], square[half:]], axis=1)


def unpack(packed):
    width = packed.shape[1] // 2
    return jnp.concatenate([packed[:, :width], packed[:, width:]], axis=0)


def pack_kernel(core_ref, out_ref):
    for i in range(core_ref.shape[0]):
        out_ref[i] = pack(core_ref[i].astype(F32).T).astype(BF16)


def pick_kernel(ids_ref, *refs):
    pieces, out_ref, table_ref = refs[:-2], refs[-2], refs[-1]
    size = pieces[0].shape[0]
    for i, piece in enumerate(pieces):
        table_ref[pl.ds(i * size, size)] = piece[...]

    def step(k, carry):
        out_ref[k] = table_ref[jnp.maximum(ids_ref[k], 0)]
        return carry

    lax.fori_loop(0, out_ref.shape[0], step, 0, unroll=8)


def grad_kernel(slot_ref, fill_ref, left_ref, right_ref, value_ref, slice_ref, out_ref, value_scr):
    value_scr[...] = value_ref[...].astype(F32)
    lanes = lax.broadcasted_iota(jnp.int32, (1, left_ref.shape[2]), 1)

    def step(t, carry):
        slot = slot_ref[t]
        left = left_ref[t]
        right = right_ref[t]
        table = unpack(slice_ref[slot])
        projected = jnp.dot(table, left, preferred_element_type=F32)
        predicted = jnp.sum(projected * right.astype(F32), axis=0, keepdims=True)
        residual = jnp.where(lanes < fill_ref[t], predicted - value_scr[pl.ds(t, 1), :], 0.0)
        weighted = (residual * left.astype(F32)).astype(BF16)
        grad = lax.dot_general(
            right, weighted, (((1,), (1,)), ((), ())), preferred_element_type=F32
        )
        out_ref[slot] = pack(grad).astype(BF16)
        return carry

    lax.fori_loop(0, left_ref.shape[0], step, 0, unroll=8)


def sum_kernel(ids_ref, grad_ref, near_ref, far_ref, acc_ref):
    acc_ref[...] = jnp.zeros_like(acc_ref)

    def step(k, carry):
        @pl.when(ids_ref[k] >= 0)
        def _():
            acc_ref[ids_ref[k]] += grad_ref[k].astype(F32)

        return carry

    lax.fori_loop(0, grad_ref.shape[0], step, 0, unroll=4)
    half = near_ref.shape[0]
    near_ref[...] = acc_ref[:half]
    far_ref[...] = acc_ref[half:].astype(BF16)


def join_kernel(near_ref, other_ref, keep_ref, *send_refs):
    size = keep_ref.shape[0]
    keep_ref[...] = near_ref[:size] + other_ref[:size].astype(F32)
    for i, send_ref in enumerate(send_refs):
        rows = pl.ds((i + 1) * size, size)
        send_ref[...] = (near_ref[rows] + other_ref[rows].astype(F32)).astype(BF16)


def update_kernel(table_ref, keep_ref, *refs):
    parts, packed_ref, out_ref = refs[:-2], refs[-2], refs[-1]
    total = keep_ref[...]
    for part in parts:
        total += part[...].astype(F32)
    packed_ref[...] = (table_ref[...].astype(F32) - total).astype(BF16)
    for i in range(out_ref.shape[0]):
        out_ref[i] = unpack(packed_ref[i].astype(F32)).T.astype(BF16)


def refresh_kernel(slot_ref, left_ref, slice_ref, out_ref):
    def step(t, carry):
        table = unpack(slice_ref[slot_ref[t]])
        out_ref[t] = jnp.dot(table, left_ref[t], preferred_element_type=F32).astype(BF16)
        return carry

    lax.fori_loop(0, left_ref.shape[0], step, 0, unroll=8)


def call(kernel, in_specs, outs, scratch=(), flops=10**6, moved=4 * 10**6):
    many = isinstance(outs, tuple)
    return pl.pallas_call(
        kernel,
        out_shape=outs,
        in_specs=in_specs,
        out_specs=(VMEM,) * len(outs) if many else VMEM,
        scratch_shapes=list(scratch),
        cost_estimate=pl.CostEstimate(flops=flops, bytes_accessed=moved, transcendentals=0),
    )


def exchange(x, axis):
    return lax.all_to_all(x, axis, split_axis=0, concat_axis=0, tiled=True)


def shift(x, groups, step):
    return lax.ppermute(x, "grp", [(g, (g + 2 * step) % groups) for g in range(groups)])


def swap(x, groups):
    return lax.ppermute(x, "grp", [(g, g ^ 1) for g in range(groups)])


def spread(mine, groups):
    near = [mine] + [shift(mine, groups, -k) for k in range(1, groups // 2)]
    return near + [swap(piece, groups) for piece in near]


def body(left, right, values, core, tile_slice, tile_fill):
    owners = lax.axis_size("own")
    groups = lax.axis_size("grp")
    chips = groups // 2
    me = lax.axis_index("grp")
    tiles, rows, rank = left.shape
    per_device = core.shape[0]
    local_count = groups * per_device
    slots = 2 * owners
    packed_shape = (rank // 2, 2 * rank)

    block = tile_slice // per_device
    owner = block % owners
    group = block // owners
    side = (group % 2) ^ (me % 2)
    away = (group // 2 - me // 2) % chips
    local = (side * chips + away) * per_device + tile_slice % per_device
    position = jnp.arange(tiles)
    same = (owner[:, None] == owner[None, :]) & (position[None, :] < position[:, None])
    slot = 2 * owner + jnp.sum(same.astype(jnp.int32), axis=1)
    hit = slot[None, :] == jnp.arange(slots)[:, None]
    wanted = jnp.max(jnp.where(hit, local[None, :], -1), axis=1)

    left_t = jnp.swapaxes(left, 1, 2)
    right_t = jnp.swapaxes(right, 1, 2)
    sds = jax.ShapeDtypeStruct
    slot_sds = sds((slots,) + packed_shape, BF16)
    mine_sds = sds((per_device,) + packed_shape, BF16)
    keep_sds = sds((per_device,) + packed_shape, F32)
    table_scr = pltpu.VMEM((local_count,) + packed_shape, BF16)
    pick = call(pick_kernel, [SMEM] + [VMEM] * groups, slot_sds, [table_scr])

    mine = call(pack_kernel, [VMEM], mine_sds)(core)
    ids = exchange(wanted.reshape(owners, 2), "own").reshape(slots)
    got = exchange(pick(ids, *spread(mine, groups)), "own")
    grads = call(
        grad_kernel,
        [SMEM, SMEM, VMEM, VMEM, VMEM, VMEM],
        slot_sds,
        [pltpu.VMEM((tiles, rows), F32)],
    )(slot, tile_fill, left_t, right_t, values, got)
    got_grads = exchange(grads, "own")
    near, far = call(
        sum_kernel,
        [SMEM, VMEM],
        (
            sds((local_count // 2,) + packed_shape, F32),
            sds((local_count // 2,) + packed_shape, BF16),
        ),
        [pltpu.VMEM((local_count,) + packed_shape, F32)],
    )(ids, got_grads)
    keep, *send = call(join_kernel, [VMEM] * 2, (keep_sds,) + (mine_sds,) * (chips - 1))(
        near, swap(far, groups)
    )
    parts = [shift(x, groups, k + 1) for k, x in enumerate(send)]
    new_mine, new_core = call(
        update_kernel, [VMEM] * (chips + 1), (mine_sds, sds(core.shape, BF16))
    )(mine, keep, *parts)
    new_got = exchange(pick(ids, *spread(new_mine, groups)), "own")
    new_left_t = call(refresh_kernel, [SMEM, VMEM, VMEM], sds(left_t.shape, BF16))(
        slot, left_t, new_got
    )
    return (new_core, jnp.swapaxes(new_left_t, 1, 2))


def solution(mesh):
    spec3 = P(("grp", "own"), None, None)
    spec2 = P(("grp", "own"), None)
    spec1 = P(("grp", "own"))
    return jax.shard_map(
        body,
        mesh=mesh,
        in_specs=(spec3, spec3, spec2, spec3, spec1, spec1),
        out_specs=(spec3, spec3),
        check_vma=False,
    )
```

```python
import functools

import jax
import jax.numpy as jnp
from jax import lax
from jax.experimental import pallas as pl
from jax.experimental.pallas import tpu as pltpu
from jax.sharding import PartitionSpec as P


VMEM = pl.BlockSpec(memory_space=pltpu.VMEM)
SMEM = pl.BlockSpec(memory_space=pltpu.SMEM)
BF16 = jnp.bfloat16
F32 = jnp.float32


def pack(square):
    half = square.shape[0] // 2
    return jnp.concatenate([square[:half], square[half:]], axis=1)


def unpack(packed):
    width = packed.shape[1] // 2
    return jnp.concatenate([packed[:, :width], packed[:, width:]], axis=0)


def pack_kernel(core_ref, out_ref):
    for i in range(core_ref.shape[0]):
        out_ref[i] = pack(core_ref[i].astype(F32).T).astype(BF16)


def index_kernel(owners, groups, per_device, tile_slice_ref, slot_ref, wanted_ref, count_ref):
    dead = groups * per_device

    def clear(c, carry):
        count_ref[c] = 0
        wanted_ref[c, 0, 0] = dead
        wanted_ref[c, 0, 1] = dead
        return carry

    def place(t, carry):
        block = tile_slice_ref[t] // per_device
        owner = block % owners
        group = block // owners
        rank = count_ref[owner]
        count_ref[owner] = rank + 1
        slot_ref[t] = 2 * owner + rank
        wanted_ref[owner, 0, rank] = group * per_device + tile_slice_ref[t] % per_device
        return carry

    lax.fori_loop(0, owners, clear, 0, unroll=8)
    lax.fori_loop(0, slot_ref.shape[0], place, 0, unroll=4)


def pick_rows(ids_ref, table_ref, out_ref):
    table_ref[table_ref.shape[0] - 1] = jnp.zeros(table_ref.shape[1:], BF16)

    def step(k, carry):
        rows = [table_ref[ids_ref[4 * k + i // 2, 0, i % 2]] for i in range(8)]
        for i, row in enumerate(rows):
            out_ref[8 * k + i] = row
        return carry

    lax.fori_loop(0, out_ref.shape[0] // 8, step, 0, unroll=2)


def rotated_kernel(me_ref, ids_ref, *refs):
    pieces, out_ref, table_ref = refs[:-2], refs[-2], refs[-1]
    groups, size = len(pieces), pieces[0].shape[0]
    for i, piece in enumerate(pieces):
        core, step = divmod(i, groups // 2)
        place = lax.rem((me_ref[0] ^ core) + 2 * step, groups)
        table_ref[pl.ds(place * size, size)] = piece[...]
    pick_rows(ids_ref, table_ref, out_ref)


def sided_kernel(me_ref, ids_ref, near_ref, far_ref, out_ref, table_ref):
    size = near_ref.shape[1]
    side = lax.rem(me_ref[0], 2)
    for x in range(near_ref.shape[0]):
        table_ref[pl.ds((2 * x + side) * size, size)] = near_ref[x]
        table_ref[pl.ds((2 * x + 1 - side) * size, size)] = far_ref[x]
    pick_rows(ids_ref, table_ref, out_ref)


def grad_kernel(slot_ref, fill_ref, left_ref, right_ref, value_ref, slice_ref, out_ref, value_scr):
    value_scr[...] = value_ref[...].astype(F32)
    lanes = lax.broadcasted_iota(jnp.int32, (1, left_ref.shape[2]), 1)
    wide = 8

    def step(k, carry):
        tiles = [wide * k + i for i in range(wide)]
        slots = [slot_ref[t] for t in tiles]
        projected = [
            jnp.dot(unpack(slice_ref[slot]), left_ref[t], preferred_element_type=F32)
            for t, slot in zip(tiles, slots)
        ]
        grads = []
        for t, proj in zip(tiles, projected):
            predicted = jnp.sum(proj * right_ref[t].astype(F32), axis=0, keepdims=True)
            residual = jnp.where(
                lanes < fill_ref[t], predicted - value_scr[pl.ds(t, 1), :], 0.0
            )
            weighted = (residual * left_ref[t].astype(F32)).astype(BF16)
            grads.append(
                lax.dot_general(
                    right_ref[t],
                    weighted,
                    (((1,), (1,)), ((), ())),
                    preferred_element_type=F32,
                )
            )
        for slot, grad in zip(slots, grads):
            out_ref[slot] = pack(grad).astype(BF16)
        return carry

    lax.fori_loop(0, left_ref.shape[0] // wide, step, 0)


def sum_kernel(ids_ref, grad_ref, me_ref, near_ref, far_ref, acc_ref):
    acc_ref[...] = jnp.zeros_like(acc_ref)

    def step(c, carry):
        for r in range(2):
            acc_ref[ids_ref[c, 0, r]] += grad_ref[2 * c + r].astype(F32)
        return carry

    lax.fori_loop(0, grad_ref.shape[0] // 2, step, 0, unroll=4)
    per_device = near_ref.shape[1]
    side = lax.rem(me_ref[0], 2)
    for x in range(near_ref.shape[0]):
        near_ref[x] = acc_ref[pl.ds((2 * x + side) * per_device, per_device)]
        far_ref[x] = acc_ref[pl.ds((2 * x + 1 - side) * per_device, per_device)].astype(BF16)


def join_kernel(near_ref, other_ref, out_ref):
    out_ref[...] = (near_ref[...] + other_ref[...].astype(F32)).astype(BF16)


def update_kernel(table_ref, part_ref, packed_ref, out_ref):
    total = jnp.sum(part_ref[...].astype(F32), axis=0)
    packed = (table_ref[...].astype(F32) - total).astype(BF16)
    for x in range(packed_ref.shape[0]):
        packed_ref[x] = packed
    for i in range(out_ref.shape[0]):
        out_ref[i] = unpack(packed[i].astype(F32)).T.astype(BF16)


def refresh_kernel(slot_ref, left_ref, slice_ref, out_ref):
    wide = 8

    def step(k, carry):
        tiles = [wide * k + i for i in range(wide)]
        fresh = [
            jnp.dot(unpack(slice_ref[slot_ref[t]]), left_ref[t], preferred_element_type=F32)
            for t in tiles
        ]
        for t, value in zip(tiles, fresh):
            out_ref[t] = value.astype(BF16)
        return carry

    lax.fori_loop(0, left_ref.shape[0] // wide, step, 0)


def call(kernel, in_specs, outs, scratch=(), out_specs=None, flops=10**6, moved=4 * 10**6):
    many = isinstance(outs, tuple)
    return pl.pallas_call(
        kernel,
        out_shape=outs,
        in_specs=in_specs,
        out_specs=out_specs or ((VMEM,) * len(outs) if many else VMEM),
        scratch_shapes=list(scratch),
        cost_estimate=pl.CostEstimate(flops=flops, bytes_accessed=moved, transcendentals=0),
    )


def exchange(x, axis):
    return lax.all_to_all(x, axis, split_axis=0, concat_axis=0, tiled=True)


def shift(x, groups, step):
    return lax.ppermute(x, "grp", [(g, (g + 2 * step) % groups) for g in range(groups)])


def swap(x, groups):
    return lax.ppermute(x, "grp", [(g, g ^ 1) for g in range(groups)])


def spread(mine, groups):
    near = [mine] + [shift(mine, groups, -k) for k in range(1, groups // 2)]
    return near + [swap(piece, groups) for piece in near]


def body(left, right, values, core, tile_slice, tile_fill):
    owners = lax.axis_size("own")
    groups = lax.axis_size("grp")
    chips = groups // 2
    tiles, rows, rank = left.shape
    per_device = core.shape[0]
    local_count = groups * per_device
    slots = 2 * owners
    packed_shape = (rank // 2, 2 * rank)
    along_x = [[2 * x + side for x in range(chips)] for side in range(2)]

    left_t = jnp.swapaxes(left, 1, 2)
    right_t = jnp.swapaxes(right, 1, 2)
    sds = jax.ShapeDtypeStruct
    slot_sds = sds((slots,) + packed_shape, BF16)
    mine_sds = sds((per_device,) + packed_shape, BF16)
    chip_shape = (chips, per_device) + packed_shape
    table_scr = pltpu.VMEM((local_count + 1,) + packed_shape, BF16)

    def exchange_x(x):
        return lax.all_to_all(
            x, "grp", split_axis=0, concat_axis=0, tiled=True, axis_index_groups=along_x
        )

    me = lax.axis_index("grp").astype(jnp.int32).reshape(1)

    slot, wanted = call(
        functools.partial(index_kernel, owners, groups, per_device),
        [SMEM],
        (sds((tiles,), jnp.int32), sds((owners, 1, 128), jnp.int32)),
        [pltpu.SMEM((owners,), jnp.int32)],
        (SMEM, SMEM),
    )(tile_slice)
    ids = exchange(wanted, "own")
    mine = call(pack_kernel, [VMEM], mine_sds)(core)
    pieces = spread(mine, groups)
    outgoing = call(
        rotated_kernel, [SMEM] * 2 + [VMEM] * groups, slot_sds, [table_scr]
    )(me, ids, *pieces)
    got = exchange(outgoing, "own")
    grads = call(
        grad_kernel,
        [SMEM, SMEM, VMEM, VMEM, VMEM, VMEM],
        slot_sds,
        [pltpu.VMEM((tiles, rows), F32)],
    )(slot, tile_fill, left_t, right_t, values, got)
    got_grads = exchange(grads, "own")
    near, far = call(
        sum_kernel,
        [SMEM, VMEM, SMEM],
        (sds(chip_shape, F32), sds(chip_shape, BF16)),
        [pltpu.VMEM((local_count + 1,) + packed_shape, F32)],
    )(ids, got_grads, me)
    joined = call(join_kernel, [VMEM] * 2, sds(chip_shape, BF16))(near, swap(far, groups))
    new_spread, new_core = call(
        update_kernel, [VMEM] * 2, (sds(chip_shape, BF16), sds(core.shape, BF16))
    )(mine, exchange_x(joined))
    new_near = exchange_x(new_spread)
    new_far = swap(new_near, groups)
    outgoing = call(sided_kernel, [SMEM, SMEM, VMEM, VMEM], slot_sds, [table_scr])(
        me, ids, new_near, new_far
    )
    new_got = exchange(outgoing, "own")
    new_left_t = call(refresh_kernel, [SMEM, VMEM, VMEM], sds(left_t.shape, BF16))(
        slot, left_t, new_got
    )
    return (new_core, jnp.swapaxes(new_left_t, 1, 2))


def solution(mesh):
    spec3 = P(("grp", "own"), None, None)
    spec2 = P(("grp", "own"), None)
    spec1 = P(("grp", "own"))
    return jax.shard_map(
        body,
        mesh=mesh,
        in_specs=(spec3, spec3, spec2, spec3, spec1, spec1),
        out_specs=(spec3, spec3),
        check_vma=False,
    )
```

```python
import functools

import jax
import jax.numpy as jnp
from jax import lax
from jax.experimental import pallas as pl
from jax.experimental.pallas import tpu as pltpu
from jax.sharding import PartitionSpec as P


VMEM = pl.BlockSpec(memory_space=pltpu.VMEM)
SMEM = pl.BlockSpec(memory_space=pltpu.SMEM)
BF16 = jnp.bfloat16
F32 = jnp.float32
WIDE = 8


def pack(block):
    half = block.shape[0] // 2
    return jnp.concatenate([block[:half], block[half:]], axis=1)


def unpack(packed):
    width = packed.shape[1] // 2
    return jnp.concatenate([packed[:, :width], packed[:, width:]], axis=0)


def pack_both(square):
    half = square.shape[0] // 2
    return jnp.concatenate([pack(square[:half]), pack(square[half:])], axis=0)


def unpack_both(packed):
    half = packed.shape[0] // 2
    return jnp.concatenate([unpack(packed[:half]), unpack(packed[half:])], axis=0)


def index_kernel(owners, groups, per_device, tile_slice_ref, slot_ref, wanted_ref, count_ref):
    dead = groups * per_device

    def clear(c, carry):
        count_ref[c] = 0
        wanted_ref[c, 0, 0] = dead
        wanted_ref[c, 0, 1] = dead
        return carry

    def place(t, carry):
        block = lax.div(tile_slice_ref[t], per_device)
        owner = lax.rem(block, owners)
        group = lax.div(block, owners)
        rank = count_ref[owner]
        count_ref[owner] = rank + 1
        slot_ref[t] = 2 * owner + rank
        wanted_ref[owner, 0, rank] = group * per_device + tile_slice_ref[t] - block * per_device
        return carry

    lax.fori_loop(0, owners, clear, 0, unroll=8)
    lax.fori_loop(0, slot_ref.shape[0], place, 0, unroll=8)


def pack_kernel(me_ref, core_ref, other_ref, out_ref):
    size = core_ref.shape[0]
    side = lax.rem(me_ref[0], 2)
    for i in range(size):
        out_ref[side * size + i] = pack_both(core_ref[i].astype(F32).T).astype(BF16)
        out_ref[(1 - side) * size + i] = pack_both(other_ref[i].astype(F32).T).astype(BF16)


def pick_kernel(me_ref, ids_ref, *refs):
    pieces, out_ref, table_ref = refs[:-2], refs[-2], refs[-1]
    chips, size = len(pieces), pieces[0].shape[0]
    for k, piece in enumerate(pieces):
        place = lax.rem(lax.div(me_ref[0], 2) + k, chips)
        table_ref[pl.ds(place * size, size)] = piece[...]
    table_ref[chips * size] = jnp.zeros(table_ref.shape[1:], BF16)

    def step(k, carry):
        rows = [table_ref[ids_ref[4 * k + i // 2, 0, i % 2]] for i in range(8)]
        for i, row in enumerate(rows):
            out_ref[8 * k + i] = row
        return carry

    lax.fori_loop(0, out_ref.shape[0] // 8, step, 0, unroll=2)


def gradient_half(half, right, left, residual):
    weighted = (residual * left.astype(F32)).astype(BF16)
    rows = right.shape[0] // 2
    return lax.dot_general(
        right[half * rows : (half + 1) * rows],
        weighted,
        (((1,), (1,)), ((), ())),
        preferred_element_type=F32,
    )


def first_kernel(slot_ref, fill_ref, left_ref, right_ref, value_ref, slice_ref, out_ref, res_ref, value_scr):
    value_scr[...] = value_ref[...].astype(F32)
    lanes = lax.broadcasted_iota(jnp.int32, (1, left_ref.shape[2]), 1)

    def step(k, carry):
        tiles = [WIDE * k + i for i in range(WIDE)]
        slots = [slot_ref[t] for t in tiles]
        projected = [
            jnp.dot(unpack_both(slice_ref[slot]), left_ref[t], preferred_element_type=F32)
            for t, slot in zip(tiles, slots)
        ]
        grads = []
        for t, proj in zip(tiles, projected):
            predicted = jnp.sum(proj * right_ref[t].astype(F32), axis=0, keepdims=True)
            residual = jnp.where(
                lanes < fill_ref[t], predicted - value_scr[pl.ds(t, 1), :], 0.0
            )
            res_ref[pl.ds(t, 1), :] = residual
            grads.append(gradient_half(0, right_ref[t], left_ref[t], residual))
        for slot, grad in zip(slots, grads):
            out_ref[slot] = pack(grad).astype(BF16)
        return carry

    lax.fori_loop(0, left_ref.shape[0] // WIDE, step, 0)


def other_kernel(slot_ref, left_ref, right_ref, res_ref, out_ref):
    def step(k, carry):
        tiles = [WIDE * k + i for i in range(WIDE)]
        grads = [
            gradient_half(1, right_ref[t], left_ref[t], res_ref[pl.ds(t, 1), :]) for t in tiles
        ]
        for t, grad in zip(tiles, grads):
            out_ref[slot_ref[t]] = pack(grad).astype(BF16)
        return carry

    lax.fori_loop(0, left_ref.shape[0] // WIDE, step, 0)


def sum_kernel(chips, me_ref, ids_ref, grad_ref, out_ref, acc_ref):
    acc_ref[...] = jnp.zeros_like(acc_ref)

    def step(c, carry):
        for r in range(2):
            acc_ref[ids_ref[c, 0, r]] += grad_ref[2 * c + r].astype(F32)
        return carry

    lax.fori_loop(0, grad_ref.shape[0] // 2, step, 0, unroll=4)
    size = out_ref.shape[0] // chips
    for k in range(chips):
        place = lax.rem(lax.div(me_ref[0], 2) + k, chips)
        out_ref[pl.ds(k * size, size)] = acc_ref[pl.ds(place * size, size)].astype(BF16)


def join_kernel(part_ref, other_ref, keep_ref, *send_refs):
    size = keep_ref.shape[0]
    keep_ref[...] = part_ref[:size].astype(F32) + other_ref[:size].astype(F32)
    for i, send_ref in enumerate(send_refs):
        rows = pl.ds((i + 1) * size, size)
        send_ref[...] = (part_ref[rows].astype(F32) + other_ref[rows].astype(F32)).astype(BF16)


def update_kernel(half, table_ref, keep_ref, *refs):
    parts, new_ref = refs[:-1], refs[-1]
    rows = new_ref.shape[1]
    total = keep_ref[...]
    for part in parts:
        total += part[...].astype(F32)
    table = table_ref[:, half * rows : (half + 1) * rows, :]
    new_ref[...] = (table.astype(F32) - total).astype(BF16)


def core_kernel(me_ref, new_a_ref, new_b_ref, out_ref):
    size = out_ref.shape[0]
    side = lax.rem(me_ref[0], 2)
    for i in range(size):
        packed = jnp.concatenate([new_a_ref[side * size + i], new_b_ref[side * size + i]], axis=0)
        out_ref[i] = unpack_both(packed.astype(F32)).T.astype(BF16)


def refresh_kernel(slot_ref, left_ref, slice_ref, *refs):
    out_ref = refs[-1]

    def step(k, carry):
        tiles = [WIDE * k + i for i in range(WIDE)]
        fresh = [
            jnp.dot(unpack(slice_ref[slot_ref[t]]), left_ref[t], preferred_element_type=F32)
            for t in tiles
        ]
        for t, value in zip(tiles, fresh):
            out_ref[t] = value.astype(BF16)
        return carry

    lax.fori_loop(0, left_ref.shape[0] // WIDE, step, 0)


def call(kernel, in_specs, outs, scratch=(), out_specs=None):
    many = isinstance(outs, tuple)
    return pl.pallas_call(
        kernel,
        out_shape=outs,
        in_specs=in_specs,
        out_specs=out_specs or ((VMEM,) * len(outs) if many else VMEM),
        scratch_shapes=list(scratch),
        cost_estimate=pl.CostEstimate(flops=10**6, bytes_accessed=4 * 10**6, transcendentals=0),
    )


def refresh(half, slot, left_t, slices, prior=None):
    tiles, rank, rows = left_t.shape
    specs = [SMEM, VMEM, VMEM] + ([] if prior is None else [pl.BlockSpec(memory_space=pl.ANY)])
    args = (slot, left_t, slices) + (() if prior is None else (prior,))
    return pl.pallas_call(
        refresh_kernel,
        grid=(1,),
        out_shape=jax.ShapeDtypeStruct(left_t.shape, BF16),
        in_specs=specs,
        out_specs=pl.BlockSpec((tiles, rank // 2, rows), lambda i: (0, half, 0)),
        input_output_aliases={} if prior is None else {3: 0},
        cost_estimate=pl.CostEstimate(flops=10**6, bytes_accessed=3 * 10**6, transcendentals=0),
    )(*args)


def exchange(x):
    return lax.all_to_all(x, "own", split_axis=0, concat_axis=0, tiled=True)


def shift(x, groups, step):
    return lax.ppermute(x, "grp", [(g, (g + 2 * step) % groups) for g in range(groups)])


def swap(x, groups):
    return lax.ppermute(x, "grp", [(g, g ^ 1) for g in range(groups)])


def spread(block, groups):
    return [block] + [shift(block, groups, -k) for k in range(1, groups // 2)]


def body(left, right, values, core, tile_slice, tile_fill):
    owners = lax.axis_size("own")
    groups = lax.axis_size("grp")
    chips = groups // 2
    tiles, rows, rank = left.shape
    per_device = core.shape[0]
    local_count = groups * per_device
    slots = 2 * owners
    sds = jax.ShapeDtypeStruct
    half_shape = (rank // 4, 2 * rank)
    full_shape = (rank // 2, 2 * rank)
    half_slots = sds((slots,) + half_shape, BF16)
    half_scr = pltpu.VMEM((local_count + 1,) + half_shape, BF16)
    full_scr = pltpu.VMEM((local_count + 1,) + full_shape, BF16)
    sum_scr = pltpu.VMEM((local_count + 1,) + half_shape, F32)
    block_sds = sds((2 * per_device,) + half_shape, BF16)
    keep_sds = sds((2 * per_device,) + half_shape, F32)
    pick_specs = [SMEM] * 2 + [VMEM] * chips

    left_t = jnp.swapaxes(left, 1, 2)
    right_t = jnp.swapaxes(right, 1, 2)
    me = lax.axis_index("grp").astype(jnp.int32).reshape(1)

    def chain(half, ids, table, got):
        part = call(
            functools.partial(sum_kernel, chips),
            [SMEM, SMEM, VMEM],
            sds((local_count,) + half_shape, BF16),
            [sum_scr],
        )(me, ids, got)
        keep, *send = call(join_kernel, [VMEM] * 2, (keep_sds,) + (block_sds,) * (chips - 1))(
            part, swap(part, groups)
        )
        parts = [shift(x, groups, k + 1) for k, x in enumerate(send)]
        new = call(
            functools.partial(update_kernel, half), [VMEM] * (chips + 1), block_sds
        )(table, keep, *parts)
        pieces = spread(new, groups)
        return new, call(pick_kernel, pick_specs, half_slots, [half_scr])(me, ids, *pieces)

    slot, wanted = call(
        functools.partial(index_kernel, owners, groups, per_device),
        [SMEM],
        (sds((tiles,), jnp.int32), sds((owners, 1, 128), jnp.int32)),
        [pltpu.SMEM((owners,), jnp.int32)],
        (SMEM, SMEM),
    )(tile_slice)
    other_core = swap(core, groups)
    ids = exchange(wanted)
    table = call(
        pack_kernel, [SMEM, VMEM, VMEM], sds((2 * per_device,) + full_shape, BF16)
    )(me, core, other_core)
    pieces = spread(table, groups)
    outgoing = call(pick_kernel, pick_specs, sds((slots,) + full_shape, BF16), [full_scr])(
        me, ids, *pieces
    )
    got = exchange(outgoing)
    grad_a, residual = call(
        first_kernel,
        [SMEM] * 2 + [VMEM] * 4,
        (half_slots, sds((tiles, rows), F32)),
        [pltpu.VMEM((tiles, rows), F32)],
    )(slot, tile_fill, left_t, right_t, values, got)
    got_a = exchange(grad_a)
    grad_b = call(other_kernel, [SMEM] + [VMEM] * 3, half_slots)(slot, left_t, right_t, residual)
    got_b = exchange(grad_b)
    new_a, out_a = chain(0, ids, table, got_a)
    slices_a = exchange(out_a)
    new_b, out_b = chain(1, ids, table, got_b)
    slices_b = exchange(out_b)
    new_left_t = refresh(0, slot, left_t, slices_a)
    new_core = call(core_kernel, [SMEM, VMEM, VMEM], sds(core.shape, BF16))(me, new_a, new_b)
    new_left_t = refresh(1, slot, left_t, slices_b, new_left_t)
    return (new_core, jnp.swapaxes(new_left_t, 1, 2))


def solution(mesh):
    spec3 = P(("grp", "own"), None, None)
    spec2 = P(("grp", "own"), None)
    spec1 = P(("grp", "own"))
    return jax.shard_map(
        body,
        mesh=mesh,
        in_specs=(spec3, spec3, spec2, spec3, spec1, spec1),
        out_specs=(spec3, spec3),
        check_vma=False,
    )
```

```python
import functools

import jax
import jax.numpy as jnp
from jax import lax
from jax.experimental import pallas as pl
from jax.experimental.pallas import tpu as pltpu
from jax.sharding import PartitionSpec as P


VMEM = pl.BlockSpec(memory_space=pltpu.VMEM)
SMEM = pl.BlockSpec(memory_space=pltpu.SMEM)
BF16 = jnp.bfloat16
F32 = jnp.float32


def pack(square):
    half = square.shape[0] // 2
    return jnp.concatenate([square[:half], square[half:]], axis=1)


def unpack(packed):
    width = packed.shape[1] // 2
    return jnp.concatenate([packed[:, :width], packed[:, width:]], axis=0)


def pack_kernel(core_ref, out_ref):
    for i in range(core_ref.shape[0]):
        out_ref[i] = pack(core_ref[i].astype(F32).T).astype(BF16)


def index_kernel(owners, groups, per_device, tile_slice_ref, slot_ref, wanted_ref, count_ref):
    dead = groups * per_device

    def clear(c, carry):
        count_ref[c] = 0
        wanted_ref[c, 0, 0] = dead
        wanted_ref[c, 0, 1] = dead
        return carry

    def place(t, carry):
        block = lax.div(tile_slice_ref[t], per_device)
        owner = lax.rem(block, owners)
        group = lax.div(block, owners)
        rank = count_ref[owner]
        count_ref[owner] = rank + 1
        slot_ref[t] = 2 * owner + rank
        wanted_ref[owner, 0, rank] = group * per_device + tile_slice_ref[t] - block * per_device
        return carry

    lax.fori_loop(0, owners, clear, 0, unroll=8)
    lax.fori_loop(0, slot_ref.shape[0], place, 0, unroll=8)


def pick_rows(ids_ref, table_ref, out_ref):
    table_ref[table_ref.shape[0] - 1] = jnp.zeros(table_ref.shape[1:], BF16)

    def step(k, carry):
        rows = [table_ref[ids_ref[4 * k + i // 2, 0, i % 2]] for i in range(8)]
        for i, row in enumerate(rows):
            out_ref[8 * k + i] = row
        return carry

    lax.fori_loop(0, out_ref.shape[0] // 8, step, 0, unroll=2)


def rotated_kernel(me_ref, ids_ref, *refs):
    pieces, out_ref, table_ref = refs[:-2], refs[-2], refs[-1]
    groups, size = len(pieces), pieces[0].shape[0]
    for i, piece in enumerate(pieces):
        core, step = divmod(i, groups // 2)
        place = lax.rem((me_ref[0] ^ core) + 2 * step, groups)
        table_ref[pl.ds(place * size, size)] = piece[...]
    pick_rows(ids_ref, table_ref, out_ref)


def sided_kernel(me_ref, ids_ref, near_ref, far_ref, out_ref, table_ref):
    size = near_ref.shape[1]
    side = lax.rem(me_ref[0], 2)
    for x in range(near_ref.shape[0]):
        table_ref[pl.ds((2 * x + side) * size, size)] = near_ref[x]
        table_ref[pl.ds((2 * x + 1 - side) * size, size)] = far_ref[x]
    pick_rows(ids_ref, table_ref, out_ref)


def grad_kernel(slot_ref, fill_ref, left_ref, right_ref, value_ref, slice_ref, out_ref, value_scr):
    value_scr[...] = value_ref[...].astype(F32)
    lanes = lax.broadcasted_iota(jnp.int32, (1, left_ref.shape[2]), 1)
    wide = 8

    def step(k, carry):
        tiles = [wide * k + i for i in range(wide)]
        slots = [slot_ref[t] for t in tiles]
        projected = [
            jnp.dot(unpack(slice_ref[slot]), left_ref[t], preferred_element_type=F32)
            for t, slot in zip(tiles, slots)
        ]
        grads = []
        for t, proj in zip(tiles, projected):
            predicted = jnp.sum(proj * right_ref[t].astype(F32), axis=0, keepdims=True)
            residual = jnp.where(
                lanes < fill_ref[t], predicted - value_scr[pl.ds(t, 1), :], 0.0
            )
            weighted = (residual * left_ref[t].astype(F32)).astype(BF16)
            grads.append(
                lax.dot_general(
                    right_ref[t],
                    weighted,
                    (((1,), (1,)), ((), ())),
                    preferred_element_type=F32,
                )
            )
        for slot, grad in zip(slots, grads):
            out_ref[slot] = pack(grad).astype(BF16)
        return carry

    lax.fori_loop(0, left_ref.shape[0] // wide, step, 0)


def sum_kernel(ids_ref, grad_ref, me_ref, near_ref, far_ref, acc_ref):
    acc_ref[...] = jnp.zeros_like(acc_ref)

    def step(c, carry):
        for r in range(2):
            acc_ref[ids_ref[c, 0, r]] += grad_ref[2 * c + r].astype(F32)
        return carry

    lax.fori_loop(0, grad_ref.shape[0] // 2, step, 0, unroll=4)
    per_device = near_ref.shape[1]
    side = lax.rem(me_ref[0], 2)
    for x in range(near_ref.shape[0]):
        near_ref[x] = acc_ref[pl.ds((2 * x + side) * per_device, per_device)]
        far_ref[x] = acc_ref[pl.ds((2 * x + 1 - side) * per_device, per_device)].astype(BF16)


def join_kernel(near_ref, other_ref, out_ref):
    out_ref[...] = (near_ref[...] + other_ref[...].astype(F32)).astype(BF16)


def update_kernel(table_ref, part_ref, packed_ref, out_ref):
    total = jnp.sum(part_ref[...].astype(F32), axis=0)
    packed = (table_ref[...].astype(F32) - total).astype(BF16)
    for x in range(packed_ref.shape[0]):
        packed_ref[x] = packed
    for i in range(out_ref.shape[0]):
        out_ref[i] = unpack(packed[i].astype(F32)).T.astype(BF16)


def refresh_kernel(slot_ref, left_ref, slice_ref, out_ref):
    wide = 8

    def step(k, carry):
        tiles = [wide * k + i for i in range(wide)]
        fresh = [
            jnp.dot(unpack(slice_ref[slot_ref[t]]), left_ref[t], preferred_element_type=F32)
            for t in tiles
        ]
        for t, value in zip(tiles, fresh):
            out_ref[t] = value.astype(BF16)
        return carry

    lax.fori_loop(0, left_ref.shape[0] // wide, step, 0)


def call(kernel, in_specs, outs, scratch=(), out_specs=None, keep=True):
    many = isinstance(outs, tuple)
    outs = outs if many else (outs,)
    specs = out_specs or (VMEM,) * len(outs)
    shapes = tuple(
        pltpu.VMEM(out.shape, out.dtype) if keep and spec is VMEM else out
        for out, spec in zip(outs, specs)
    )
    run = pl.pallas_call(
        kernel,
        out_shape=shapes,
        in_specs=in_specs,
        out_specs=tuple(specs),
        scratch_shapes=list(scratch),
        compiler_params=pltpu.CompilerParams(vmem_limit_bytes=12 * 2**20),
        cost_estimate=pl.CostEstimate(flops=10**6, bytes_accessed=4 * 10**6, transcendentals=0),
    )

    def place(*args):
        placed = [
            pltpu.with_memory_space_constraint(arg, pltpu.VMEM) if spec is VMEM else arg
            for arg, spec in zip(args, in_specs)
        ]
        results = run(*placed)
        return results if many else results[0]

    return place


def exchange(x, axis):
    return lax.all_to_all(x, axis, split_axis=0, concat_axis=0, tiled=True)


def shift(x, groups, step):
    return lax.ppermute(x, "grp", [(g, (g + 2 * step) % groups) for g in range(groups)])


def swap(x, groups):
    return lax.ppermute(x, "grp", [(g, g ^ 1) for g in range(groups)])


def spread(mine, groups):
    near = [mine] + [shift(mine, groups, -k) for k in range(1, groups // 2)]
    return near + [swap(piece, groups) for piece in near]


def body(left, right, values, core, tile_slice, tile_fill):
    owners = lax.axis_size("own")
    groups = lax.axis_size("grp")
    chips = groups // 2
    tiles, rows, rank = left.shape
    per_device = core.shape[0]
    local_count = groups * per_device
    slots = 2 * owners
    packed_shape = (rank // 2, 2 * rank)
    along_x = [[2 * x + side for x in range(chips)] for side in range(2)]

    left_t = jnp.swapaxes(left, 1, 2)
    right_t = jnp.swapaxes(right, 1, 2)
    sds = jax.ShapeDtypeStruct
    slot_sds = sds((slots,) + packed_shape, BF16)
    mine_sds = sds((per_device,) + packed_shape, BF16)
    chip_shape = (chips, per_device) + packed_shape
    table_scr = pltpu.VMEM((local_count + 1,) + packed_shape, BF16)

    def exchange_x(x):
        return lax.all_to_all(
            x, "grp", split_axis=0, concat_axis=0, tiled=True, axis_index_groups=along_x
        )

    me = lax.axis_index("grp").astype(jnp.int32).reshape(1)

    slot, wanted = call(
        functools.partial(index_kernel, owners, groups, per_device),
        [SMEM],
        (sds((tiles,), jnp.int32), sds((owners, 1, 128), jnp.int32)),
        [pltpu.SMEM((owners,), jnp.int32)],
        (SMEM, SMEM),
    )(tile_slice)
    ids = exchange(wanted, "own")
    mine = call(pack_kernel, [VMEM], mine_sds)(core)
    pieces = spread(mine, groups)
    outgoing = call(
        rotated_kernel, [SMEM] * 2 + [VMEM] * groups, slot_sds, [table_scr]
    )(me, ids, *pieces)
    got = exchange(outgoing, "own")
    grads = call(
        grad_kernel,
        [SMEM, SMEM, VMEM, VMEM, VMEM, VMEM],
        slot_sds,
        [pltpu.VMEM((tiles, rows), F32)],
    )(slot, tile_fill, left_t, right_t, values, got)
    got_grads = exchange(grads, "own")
    near, far = call(
        sum_kernel,
        [SMEM, VMEM, SMEM],
        (sds(chip_shape, F32), sds(chip_shape, BF16)),
        [pltpu.VMEM((local_count + 1,) + packed_shape, F32)],
    )(ids, got_grads, me)
    joined = call(join_kernel, [VMEM] * 2, sds(chip_shape, BF16))(near, swap(far, groups))
    new_spread, new_core = call(
        update_kernel, [VMEM] * 2, (sds(chip_shape, BF16), sds(core.shape, BF16))
    )(mine, exchange_x(joined))
    new_near = exchange_x(new_spread)
    new_far = swap(new_near, groups)
    outgoing = call(sided_kernel, [SMEM, SMEM, VMEM, VMEM], slot_sds, [table_scr])(
        me, ids, new_near, new_far
    )
    new_got = exchange(outgoing, "own")
    new_left_t = call(refresh_kernel, [SMEM, VMEM, VMEM], sds(left_t.shape, BF16), keep=False)(
        slot, left_t, new_got
    )
    return (new_core, jnp.swapaxes(new_left_t, 1, 2))


def solution(mesh):
    spec3 = P(("grp", "own"), None, None)
    spec2 = P(("grp", "own"), None)
    spec1 = P(("grp", "own"))
    return jax.shard_map(
        body,
        mesh=mesh,
        in_specs=(spec3, spec3, spec2, spec3, spec1, spec1),
        out_specs=(spec3, spec3),
        check_vma=False,
    )
```

```python
import functools

import jax
import jax.numpy as jnp
from jax import lax
from jax.experimental import pallas as pl
from jax.experimental.pallas import tpu as pltpu
from jax.sharding import PartitionSpec as P


VMEM = pl.BlockSpec(memory_space=pltpu.VMEM)
SMEM = pl.BlockSpec(memory_space=pltpu.SMEM)
BF16 = jnp.bfloat16
F32 = jnp.float32


def pack(square):
    half = square.shape[0] // 2
    return jnp.concatenate([square[:half], square[half:]], axis=1)


def unpack(packed):
    width = packed.shape[1] // 2
    return jnp.concatenate([packed[:, :width], packed[:, width:]], axis=0)


def pack_kernel(core_ref, out_ref):
    for i in range(core_ref.shape[0]):
        out_ref[i] = pack(core_ref[i].astype(F32).T).astype(BF16)


def index_kernel(owners, groups, per_device, tile_slice_ref, slot_ref, wanted_ref, count_ref):
    dead = groups * per_device

    def clear(c, carry):
        count_ref[c] = 0
        wanted_ref[c, 0, 0] = dead
        wanted_ref[c, 0, 1] = dead
        return carry

    def place(t, carry):
        block = lax.div(tile_slice_ref[t], per_device)
        owner = lax.rem(block, owners)
        group = lax.div(block, owners)
        rank = count_ref[owner]
        count_ref[owner] = rank + 1
        slot_ref[t] = 2 * owner + rank
        wanted_ref[owner, 0, rank] = group * per_device + tile_slice_ref[t] - block * per_device
        return carry

    lax.fori_loop(0, owners, clear, 0, unroll=8)
    lax.fori_loop(0, slot_ref.shape[0], place, 0, unroll=8)


def pick_rows(ids_ref, table_ref, out_ref):
    table_ref[table_ref.shape[0] - 1] = jnp.zeros(table_ref.shape[1:], BF16)

    def step(k, carry):
        rows = [table_ref[ids_ref[4 * k + i // 2, 0, i % 2]] for i in range(8)]
        for i, row in enumerate(rows):
            out_ref[8 * k + i] = row
        return carry

    lax.fori_loop(0, out_ref.shape[0] // 8, step, 0, unroll=2)


def bundle_kernel(*refs):
    pieces, out_ref = refs[:-1], refs[-1]
    for k, piece in enumerate(pieces):
        out_ref[k] = piece[...]


def sided_kernel(turned, me_ref, ids_ref, near_ref, far_ref, out_ref, table_ref):
    chips, size = near_ref.shape[:2]
    side = lax.rem(me_ref[0], 2)
    turn = lax.div(me_ref[0], 2) if turned else 0
    for x in range(chips):
        place = 2 * lax.rem(turn + x, chips)
        table_ref[pl.ds((place + side) * size, size)] = near_ref[x]
        table_ref[pl.ds((place + 1 - side) * size, size)] = far_ref[x]
    pick_rows(ids_ref, table_ref, out_ref)


def grad_kernel(slot_ref, fill_ref, left_ref, right_ref, value_ref, slice_ref, out_ref, value_scr):
    value_scr[...] = value_ref[...].astype(F32)
    lanes = lax.broadcasted_iota(jnp.int32, (1, left_ref.shape[2]), 1)
    wide = 8

    def step(k, carry):
        tiles = [wide * k + i for i in range(wide)]
        slots = [slot_ref[t] for t in tiles]
        projected = [
            jnp.dot(unpack(slice_ref[slot]), left_ref[t], preferred_element_type=F32)
            for t, slot in zip(tiles, slots)
        ]
        grads = []
        for t, proj in zip(tiles, projected):
            predicted = jnp.sum(proj * right_ref[t].astype(F32), axis=0, keepdims=True)
            residual = jnp.where(
                lanes < fill_ref[t], predicted - value_scr[pl.ds(t, 1), :], 0.0
            )
            weighted = (residual * left_ref[t].astype(F32)).astype(BF16)
            grads.append(
                lax.dot_general(
                    right_ref[t],
                    weighted,
                    (((1,), (1,)), ((), ())),
                    preferred_element_type=F32,
                )
            )
        for slot, grad in zip(slots, grads):
            out_ref[slot] = pack(grad).astype(BF16)
        return carry

    lax.fori_loop(0, left_ref.shape[0] // wide, step, 0)


def sum_kernel(ids_ref, grad_ref, me_ref, near_ref, far_ref, acc_ref):
    acc_ref[...] = jnp.zeros_like(acc_ref)

    def step(c, carry):
        for r in range(2):
            acc_ref[ids_ref[c, 0, r]] += grad_ref[2 * c + r].astype(F32)
        return carry

    lax.fori_loop(0, grad_ref.shape[0] // 2, step, 0, unroll=4)
    per_device = near_ref.shape[1]
    side = lax.rem(me_ref[0], 2)
    for x in range(near_ref.shape[0]):
        near_ref[x] = acc_ref[pl.ds((2 * x + side) * per_device, per_device)]
        far_ref[x] = acc_ref[pl.ds((2 * x + 1 - side) * per_device, per_device)].astype(BF16)


def join_kernel(near_ref, other_ref, out_ref):
    out_ref[...] = (near_ref[...] + other_ref[...].astype(F32)).astype(BF16)


def update_kernel(table_ref, part_ref, packed_ref, out_ref):
    total = jnp.sum(part_ref[...].astype(F32), axis=0)
    packed = (table_ref[...].astype(F32) - total).astype(BF16)
    for x in range(packed_ref.shape[0]):
        packed_ref[x] = packed
    for i in range(out_ref.shape[0]):
        out_ref[i] = unpack(packed[i].astype(F32)).T.astype(BF16)


def refresh_kernel(slot_ref, left_ref, slice_ref, out_ref):
    wide = 8

    def step(k, carry):
        tiles = [wide * k + i for i in range(wide)]
        fresh = [
            jnp.dot(unpack(slice_ref[slot_ref[t]]), left_ref[t], preferred_element_type=F32)
            for t in tiles
        ]
        for t, value in zip(tiles, fresh):
            out_ref[t] = value.astype(BF16)
        return carry

    lax.fori_loop(0, left_ref.shape[0] // wide, step, 0)


def call(kernel, in_specs, outs, scratch=(), out_specs=None, loose=()):
    many = isinstance(outs, tuple)
    outs = outs if many else (outs,)
    specs = out_specs or (VMEM,) * len(outs)
    shapes = tuple(
        pltpu.VMEM(out.shape, out.dtype) if spec is VMEM and i not in loose else out
        for i, (out, spec) in enumerate(zip(outs, specs))
    )
    run = pl.pallas_call(
        kernel,
        out_shape=shapes,
        in_specs=in_specs,
        out_specs=tuple(specs),
        scratch_shapes=list(scratch),
        compiler_params=pltpu.CompilerParams(vmem_limit_bytes=12 * 2**20),
        cost_estimate=pl.CostEstimate(flops=10**6, bytes_accessed=4 * 10**6, transcendentals=0),
    )

    def place(*args):
        placed = [
            pltpu.with_memory_space_constraint(arg, pltpu.VMEM) if spec is VMEM else arg
            for arg, spec in zip(args, in_specs)
        ]
        results = run(*placed)
        return results if many else results[0]

    return place


def exchange(x, axis):
    return lax.all_to_all(x, axis, split_axis=0, concat_axis=0, tiled=True)


def shift(x, groups, step):
    return lax.ppermute(x, "grp", [(g, (g + 2 * step) % groups) for g in range(groups)])


def swap(x, groups):
    return lax.ppermute(x, "grp", [(g, g ^ 1) for g in range(groups)])


def spread(mine, groups):
    return [mine] + [shift(mine, groups, -k) for k in range(1, groups // 2)]


def body(left, right, values, core, tile_slice, tile_fill):
    owners = lax.axis_size("own")
    groups = lax.axis_size("grp")
    chips = groups // 2
    tiles, rows, rank = left.shape
    per_device = core.shape[0]
    local_count = groups * per_device
    slots = 2 * owners
    packed_shape = (rank // 2, 2 * rank)
    along_x = [[2 * x + side for x in range(chips)] for side in range(2)]

    left_t = jnp.swapaxes(left, 1, 2)
    right_t = jnp.swapaxes(right, 1, 2)
    sds = jax.ShapeDtypeStruct
    slot_sds = sds((slots,) + packed_shape, BF16)
    mine_sds = sds((per_device,) + packed_shape, BF16)
    chip_shape = (chips, per_device) + packed_shape
    table_scr = pltpu.VMEM((local_count + 1,) + packed_shape, BF16)

    def exchange_x(x):
        return lax.all_to_all(
            x, "grp", split_axis=0, concat_axis=0, tiled=True, axis_index_groups=along_x
        )

    me = lax.axis_index("grp").astype(jnp.int32).reshape(1)

    slot, wanted = call(
        functools.partial(index_kernel, owners, groups, per_device),
        [SMEM],
        (sds((tiles,), jnp.int32), sds((owners, 1, 128), jnp.int32)),
        [pltpu.SMEM((owners,), jnp.int32)],
        (SMEM, SMEM),
    )(tile_slice)
    ids = exchange(wanted, "own")
    mine = call(pack_kernel, [VMEM], mine_sds)(core)
    pieces = spread(mine, groups)
    near = call(bundle_kernel, [VMEM] * chips, sds(chip_shape, BF16))(*pieces)
    outgoing = call(
        functools.partial(sided_kernel, True), [SMEM] * 2 + [VMEM] * 2, slot_sds, [table_scr]
    )(me, ids, near, swap(near, groups))
    got = exchange(outgoing, "own")
    grads = call(
        grad_kernel,
        [SMEM, SMEM, VMEM, VMEM, VMEM, VMEM],
        slot_sds,
        [pltpu.VMEM((tiles, rows), F32)],
    )(slot, tile_fill, left_t, right_t, values, got)
    got_grads = exchange(grads, "own")
    near, far = call(
        sum_kernel,
        [SMEM, VMEM, SMEM],
        (sds(chip_shape, F32), sds(chip_shape, BF16)),
        [pltpu.VMEM((local_count + 1,) + packed_shape, F32)],
    )(ids, got_grads, me)
    joined = call(join_kernel, [VMEM] * 2, sds(chip_shape, BF16))(near, swap(far, groups))
    new_spread, new_core = call(
        update_kernel, [VMEM] * 2, (sds(chip_shape, BF16), sds(core.shape, BF16)), loose=(1,)
    )(mine, exchange_x(joined))
    new_near = exchange_x(new_spread)
    new_far = swap(new_near, groups)
    outgoing = call(
        functools.partial(sided_kernel, False), [SMEM] * 2 + [VMEM] * 2, slot_sds, [table_scr])(
        me, ids, new_near, new_far
    )
    new_got = exchange(outgoing, "own")
    new_left_t = call(refresh_kernel, [SMEM, VMEM, VMEM], sds(left_t.shape, BF16), loose=(0,))(
        slot, left_t, new_got
    )
    return (new_core, jnp.swapaxes(new_left_t, 1, 2))


def solution(mesh):
    spec3 = P(("grp", "own"), None, None)
    spec2 = P(("grp", "own"), None)
    spec1 = P(("grp", "own"))
    return jax.shard_map(
        body,
        mesh=mesh,
        in_specs=(spec3, spec3, spec2, spec3, spec1, spec1),
        out_specs=(spec3, spec3),
        check_vma=False,
    )
```

```python
import functools

import jax
import jax.numpy as jnp
from jax import lax
from jax.experimental import pallas as pl
from jax.experimental.pallas import tpu as pltpu
from jax.sharding import PartitionSpec as P


VMEM = pl.BlockSpec(memory_space=pltpu.VMEM)
SMEM = pl.BlockSpec(memory_space=pltpu.SMEM)
HBM = pl.BlockSpec(memory_space=pltpu.HBM)
BF16 = jnp.bfloat16
F32 = jnp.float32


def pack(square):
    half = square.shape[0] // 2
    return jnp.concatenate([square[:half], square[half:]], axis=1)


def unpack(packed):
    width = packed.shape[1] // 2
    return jnp.concatenate([packed[:, :width], packed[:, width:]], axis=0)


def prepare_kernel(
    owners, groups, tile_slice_ref, core_ref, slot_ref, wanted_ref, out_ref, count_ref, core_scr, sem
):
    per_device = core_ref.shape[0]
    dead = groups * per_device
    fetch = pltpu.make_async_copy(core_ref, core_scr, sem)
    fetch.start()

    def clear(c, carry):
        count_ref[c] = 0
        wanted_ref[c, 0, 0] = dead
        wanted_ref[c, 0, 1] = dead
        return carry

    def place(t, carry):
        block = lax.div(tile_slice_ref[t], per_device)
        owner = lax.rem(block, owners)
        group = lax.div(block, owners)
        rank = count_ref[owner]
        count_ref[owner] = rank + 1
        slot_ref[t] = 2 * owner + rank
        wanted_ref[owner, 0, rank] = (group - block) * per_device + tile_slice_ref[t]
        return carry

    lax.fori_loop(0, owners, clear, 0, unroll=8)
    lax.fori_loop(0, slot_ref.shape[0], place, 0, unroll=8)
    fetch.wait()
    for i in range(per_device):
        out_ref[i] = pack(core_scr[i].astype(F32).T).astype(BF16)


def pick_rows(ids_ref, table_ref, out_ref):
    table_ref[table_ref.shape[0] - 1] = jnp.zeros(table_ref.shape[1:], BF16)

    def step(k, carry):
        rows = [table_ref[ids_ref[4 * k + i // 2, 0, i % 2]] for i in range(8)]
        for i, row in enumerate(rows):
            out_ref[8 * k + i] = row
        return carry

    lax.fori_loop(0, out_ref.shape[0] // 8, step, 0, unroll=2)


def bundle_kernel(*refs):
    pieces, out_ref = refs[:-1], refs[-1]
    for k, piece in enumerate(pieces):
        out_ref[k] = piece[...]


def sided_kernel(turned, me_ref, ids_ref, near_ref, far_ref, out_ref, table_ref):
    chips, size = near_ref.shape[:2]
    side = lax.rem(me_ref[0], 2)
    turn = lax.div(me_ref[0], 2) if turned else 0
    for x in range(chips):
        place = 2 * lax.rem(turn + x, chips)
        table_ref[pl.ds((place + side) * size, size)] = near_ref[x]
        table_ref[pl.ds((place + 1 - side) * size, size)] = far_ref[x]
    pick_rows(ids_ref, table_ref, out_ref)


def grad_kernel(slot_ref, fill_ref, left_ref, right_ref, value_ref, slice_ref, out_ref, value_scr):
    value_scr[...] = value_ref[...].astype(F32)
    lanes = lax.broadcasted_iota(jnp.int32, (1, left_ref.shape[2]), 1)
    wide = left_ref.shape[0]

    def step(k, carry):
        tiles = [wide * k + i for i in range(wide)]
        slots = [slot_ref[t] for t in tiles]
        projected = [
            jnp.dot(unpack(slice_ref[slot]), left_ref[t], preferred_element_type=F32)
            for t, slot in zip(tiles, slots)
        ]
        grads = []
        for t, proj in zip(tiles, projected):
            predicted = jnp.sum(proj * right_ref[t].astype(F32), axis=0, keepdims=True)
            residual = jnp.where(
                lanes < fill_ref[t], predicted - value_scr[pl.ds(t, 1), :], 0.0
            )
            weighted = (residual * left_ref[t].astype(F32)).astype(BF16)
            grads.append(
                lax.dot_general(
                    right_ref[t],
                    weighted,
                    (((1,), (1,)), ((), ())),
                    preferred_element_type=F32,
                )
            )
        for slot, grad in zip(slots, grads):
            out_ref[slot] = pack(grad).astype(BF16)
        return carry

    lax.fori_loop(0, left_ref.shape[0] // wide, step, 0)


def sum_kernel(ids_ref, grad_ref, me_ref, near_ref, far_ref, acc_ref):
    acc_ref[...] = jnp.zeros_like(acc_ref)

    def step(c, carry):
        for r in range(2):
            acc_ref[ids_ref[c, 0, r]] += grad_ref[2 * c + r].astype(F32)
        return carry

    lax.fori_loop(0, grad_ref.shape[0] // 2, step, 0, unroll=4)
    per_device = near_ref.shape[1]
    side = lax.rem(me_ref[0], 2)
    for x in range(near_ref.shape[0]):
        near_ref[x] = acc_ref[pl.ds((2 * x + side) * per_device, per_device)]
        far_ref[x] = acc_ref[pl.ds((2 * x + 1 - side) * per_device, per_device)].astype(BF16)


def join_kernel(near_ref, other_ref, out_ref):
    out_ref[...] = (near_ref[...] + other_ref[...].astype(F32)).astype(BF16)


def update_kernel(table_ref, part_ref, packed_ref, out_ref):
    total = jnp.sum(part_ref[...].astype(F32), axis=0)
    packed = (table_ref[...].astype(F32) - total).astype(BF16)
    for x in range(packed_ref.shape[0]):
        packed_ref[x] = packed
    for i in range(out_ref.shape[0]):
        out_ref[i] = unpack(packed[i].astype(F32)).T.astype(BF16)


def refresh_kernel(slot_ref, left_ref, slice_ref, out_ref):
    wide = left_ref.shape[0]

    def step(k, carry):
        tiles = [wide * k + i for i in range(wide)]
        fresh = [
            jnp.dot(unpack(slice_ref[slot_ref[t]]), left_ref[t], preferred_element_type=F32)
            for t in tiles
        ]
        for t, value in zip(tiles, fresh):
            out_ref[t] = value.astype(BF16)
        return carry

    lax.fori_loop(0, left_ref.shape[0] // wide, step, 0)


def call(kernel, in_specs, outs, scratch=(), out_specs=None, loose=()):
    many = isinstance(outs, tuple)
    outs = outs if many else (outs,)
    specs = out_specs or (VMEM,) * len(outs)
    shapes = tuple(
        pltpu.VMEM(out.shape, out.dtype) if spec is VMEM and i not in loose else out
        for i, (out, spec) in enumerate(zip(outs, specs))
    )
    run = pl.pallas_call(
        kernel,
        out_shape=shapes,
        in_specs=in_specs,
        out_specs=tuple(specs),
        scratch_shapes=list(scratch),
        compiler_params=pltpu.CompilerParams(vmem_limit_bytes=12 * 2**20),
        cost_estimate=pl.CostEstimate(flops=10**6, bytes_accessed=4 * 10**6, transcendentals=0),
    )

    def place(*args):
        placed = [
            arg if spec is SMEM else pltpu.with_memory_space_constraint(arg, spec.memory_space)
            for arg, spec in zip(args, in_specs)
        ]
        results = run(*placed)
        return results if many else results[0]

    return place


def exchange(x, axis):
    return lax.all_to_all(x, axis, split_axis=0, concat_axis=0, tiled=True)


def shift(x, groups, step):
    return lax.ppermute(x, "grp", [(g, (g + 2 * step) % groups) for g in range(groups)])


def swap(x, groups):
    return lax.ppermute(x, "grp", [(g, g ^ 1) for g in range(groups)])


def body(left, right, values, core, tile_slice, tile_fill):
    owners = lax.axis_size("own")
    groups = lax.axis_size("grp")
    chips = groups // 2
    tiles, rows, rank = left.shape
    per_device = core.shape[0]
    local_count = groups * per_device
    slots = 2 * owners
    packed_shape = (rank // 2, 2 * rank)
    along_x = [[2 * x + side for x in range(chips)] for side in range(2)]

    left_t = jnp.swapaxes(left, 1, 2)
    right_t = jnp.swapaxes(right, 1, 2)
    sds = jax.ShapeDtypeStruct
    slot_sds = sds((slots,) + packed_shape, BF16)
    mine_sds = sds((per_device,) + packed_shape, BF16)
    chip_shape = (chips, per_device) + packed_shape
    table_scr = pltpu.VMEM((local_count + 1,) + packed_shape, BF16)

    def exchange_x(x):
        return lax.all_to_all(
            x, "grp", split_axis=0, concat_axis=0, tiled=True, axis_index_groups=along_x
        )

    me = lax.axis_index("grp").astype(jnp.int32).reshape(1)

    slot, wanted, mine = call(
        functools.partial(prepare_kernel, owners, groups),
        [SMEM, HBM],
        (sds((tiles,), jnp.int32), sds((owners, 1, 128), jnp.int32), mine_sds),
        [
            pltpu.SMEM((owners,), jnp.int32),
            pltpu.VMEM(core.shape, BF16),
            pltpu.SemaphoreType.DMA,
        ],
        (SMEM, SMEM, VMEM),
    )(pltpu.with_memory_space_constraint(tile_slice, pltpu.HBM), core)
    distant = {k: shift(mine, groups, -k) for k in range(2, chips, 2)}
    ids = exchange(wanted, "own")
    adjacent = {k: shift(mine, groups, -k) for k in range(1, chips, 2)}
    pieces = [mine] + [{**distant, **adjacent}[k] for k in range(1, chips)]
    near = call(bundle_kernel, [VMEM] * chips, sds(chip_shape, BF16))(*pieces)
    outgoing = call(
        functools.partial(sided_kernel, True), [SMEM] * 2 + [VMEM] * 2, slot_sds, [table_scr]
    )(me, ids, near, swap(near, groups))
    got = exchange(outgoing, "own")
    grads = call(
        grad_kernel,
        [SMEM, SMEM, VMEM, VMEM, VMEM, VMEM],
        slot_sds,
        [pltpu.VMEM((tiles, rows), F32)],
    )(slot, tile_fill, left_t, right_t, values, got)
    got_grads = exchange(grads, "own")
    near, far = call(
        sum_kernel,
        [SMEM, VMEM, SMEM],
        (sds(chip_shape, F32), sds(chip_shape, BF16)),
        [pltpu.VMEM((local_count + 1,) + packed_shape, F32)],
    )(ids, got_grads, me)
    joined = call(join_kernel, [VMEM] * 2, sds(chip_shape, BF16))(near, swap(far, groups))
    new_spread, new_core = call(
        update_kernel, [VMEM] * 2, (sds(chip_shape, BF16), sds(core.shape, BF16)), loose=(1,)
    )(mine, exchange_x(joined))
    new_near = exchange_x(new_spread)
    new_far = swap(new_near, groups)
    outgoing = call(
        functools.partial(sided_kernel, False), [SMEM] * 2 + [VMEM] * 2, slot_sds, [table_scr])(
        me, ids, new_near, new_far
    )
    new_got = exchange(outgoing, "own")
    new_left_t = call(refresh_kernel, [SMEM, VMEM, VMEM], sds(left_t.shape, BF16), loose=(0,))(slot, left_t, new_got)
    return (new_core, jnp.swapaxes(new_left_t, 1, 2))


def solution(mesh):
    spec3 = P(("grp", "own"), None, None)
    spec2 = P(("grp", "own"), None)
    spec1 = P(("grp", "own"))
    return jax.shard_map(
        body,
        mesh=mesh,
        in_specs=(spec3, spec3, spec2, spec3, spec1, spec1),
        out_specs=(spec3, spec3),
        check_vma=False,
    )
```

```python
import functools

import jax
import jax.numpy as jnp
from jax import lax
from jax.experimental import pallas as pl
from jax.experimental.pallas import tpu as pltpu
from jax.sharding import PartitionSpec as P


VMEM = pl.BlockSpec(memory_space=pltpu.VMEM)
SMEM = pl.BlockSpec(memory_space=pltpu.SMEM)
HBM = pl.BlockSpec(memory_space=pltpu.HBM)
BF16 = jnp.bfloat16
F32 = jnp.float32
SHIFT = 16


def pack(square):
    half = square.shape[0] // 2
    return jnp.concatenate([square[:half], square[half:]], axis=1)


def unpack(packed):
    width = packed.shape[1] // 2
    return jnp.concatenate([packed[:, :width], packed[:, width:]], axis=0)


def prepare_kernel(
    owners, groups, tiles_ref, core_ref, slot_ref, wanted_ref, out_ref, core_scr, index_scr, sem, index_sem
):
    fetch_index = pltpu.make_async_copy(tiles_ref, index_scr, index_sem)
    fetch_index.start()
    fetch = pltpu.make_async_copy(core_ref, core_scr, sem)
    fetch.start()
    per_device = core_ref.shape[0]
    tiles = tiles_ref.shape[1]
    magic = -(-(2**SHIFT) // per_device)
    fetch_index.wait()
    index = index_scr[...]
    block = lax.shift_right_logical(index * magic, SHIFT)
    group = lax.shift_right_logical(block * -(-(2**SHIFT) // owners), SHIFT)
    owner = block - group * owners
    local = (group - block) * per_device + index

    mine = jnp.broadcast_to(owner.astype(F32), (tiles, tiles))
    row = lax.broadcasted_iota(jnp.int32, (tiles, tiles), 0)
    col = lax.broadcasted_iota(jnp.int32, (tiles, tiles), 1)
    earlier = jnp.where((mine == mine.T) & (row < col), 1, 0)
    slot = 2 * owner + jnp.sum(earlier, axis=0, keepdims=True)
    slot_ref[...] = slot

    dead = groups * per_device
    lane = lax.broadcasted_iota(jnp.int32, wanted_ref.shape, 1)
    seat = 2 * lax.broadcasted_iota(jnp.int32, (owners, tiles), 0)
    asked = [
        jnp.sum(jnp.where(slot == seat + r, local - dead, 0), axis=1, keepdims=True) + dead
        for r in range(2)
    ]
    wanted_ref[...] = jnp.where(lane == 0, asked[0], asked[1])
    fetch.wait()
    for i in range(per_device):
        out_ref[i] = pack(core_scr[i].astype(F32).T).astype(BF16)


def pick_rows(ids_ref, table_ref, out_ref):
    table_ref[table_ref.shape[0] - 1] = jnp.zeros(table_ref.shape[1:], BF16)

    def step(k, carry):
        rows = [table_ref[ids_ref[4 * k + i // 2, 0, i % 2]] for i in range(8)]
        for i, row in enumerate(rows):
            out_ref[8 * k + i] = row
        return carry

    lax.fori_loop(0, out_ref.shape[0] // 8, step, 0, unroll=2)


def bundle_kernel(*refs):
    pieces, out_ref = refs[:-1], refs[-1]
    for k, piece in enumerate(pieces):
        out_ref[k] = piece[...]


def sided_kernel(turned, me_ref, ids_ref, near_ref, far_ref, out_ref, table_ref):
    chips, size = near_ref.shape[:2]
    side = lax.rem(me_ref[0], 2)
    turn = lax.div(me_ref[0], 2) if turned else 0
    for x in range(chips):
        place = 2 * lax.rem(turn + x, chips)
        table_ref[pl.ds((place + side) * size, size)] = near_ref[x]
        table_ref[pl.ds((place + 1 - side) * size, size)] = far_ref[x]
    pick_rows(ids_ref, table_ref, out_ref)


def grad_kernel(slot_ref, fill_ref, left_ref, right_ref, value_ref, slice_ref, out_ref, value_scr):
    value_scr[...] = value_ref[...].astype(F32)
    lanes = lax.broadcasted_iota(jnp.int32, (1, left_ref.shape[2]), 1)
    wide = left_ref.shape[0]

    def step(k, carry):
        tiles = [wide * k + i for i in range(wide)]
        slots = [slot_ref[t] for t in tiles]
        projected = [
            jnp.dot(unpack(slice_ref[slot]), left_ref[t], preferred_element_type=F32)
            for t, slot in zip(tiles, slots)
        ]
        grads = []
        for t, proj in zip(tiles, projected):
            predicted = jnp.sum(proj * right_ref[t].astype(F32), axis=0, keepdims=True)
            residual = jnp.where(
                lanes < fill_ref[t], predicted - value_scr[pl.ds(t, 1), :], 0.0
            )
            weighted = (residual * left_ref[t].astype(F32)).astype(BF16)
            grads.append(
                lax.dot_general(
                    right_ref[t],
                    weighted,
                    (((1,), (1,)), ((), ())),
                    preferred_element_type=F32,
                )
            )
        for slot, grad in zip(slots, grads):
            out_ref[slot] = pack(grad).astype(BF16)
        return carry

    lax.fori_loop(0, left_ref.shape[0] // wide, step, 0)


def sum_kernel(ids_ref, grad_ref, me_ref, near_ref, far_ref, acc_ref):
    acc_ref[...] = jnp.zeros_like(acc_ref)

    def step(c, carry):
        for r in range(2):
            acc_ref[ids_ref[c, 0, r]] += grad_ref[2 * c + r].astype(F32)
        return carry

    lax.fori_loop(0, grad_ref.shape[0] // 2, step, 0, unroll=4)
    per_device = near_ref.shape[1]
    side = lax.rem(me_ref[0], 2)
    for x in range(near_ref.shape[0]):
        near_ref[x] = acc_ref[pl.ds((2 * x + side) * per_device, per_device)]
        far_ref[x] = acc_ref[pl.ds((2 * x + 1 - side) * per_device, per_device)].astype(BF16)


def join_kernel(near_ref, other_ref, out_ref):
    out_ref[...] = (near_ref[...] + other_ref[...].astype(F32)).astype(BF16)


def update_kernel(table_ref, part_ref, packed_ref, out_ref):
    total = jnp.sum(part_ref[...].astype(F32), axis=0)
    packed = (table_ref[...].astype(F32) - total).astype(BF16)
    for x in range(packed_ref.shape[0]):
        packed_ref[x] = packed
    for i in range(out_ref.shape[0]):
        out_ref[i] = unpack(packed[i].astype(F32)).T.astype(BF16)


def refresh_kernel(slot_ref, left_ref, slice_ref, out_ref):
    wide = left_ref.shape[0]

    def step(k, carry):
        tiles = [wide * k + i for i in range(wide)]
        fresh = [
            jnp.dot(unpack(slice_ref[slot_ref[t]]), left_ref[t], preferred_element_type=F32)
            for t in tiles
        ]
        for t, value in zip(tiles, fresh):
            out_ref[t] = value.astype(BF16)
        return carry

    lax.fori_loop(0, left_ref.shape[0] // wide, step, 0)


def call(kernel, in_specs, outs, scratch=(), out_specs=None, loose=()):
    many = isinstance(outs, tuple)
    outs = outs if many else (outs,)
    specs = out_specs or (VMEM,) * len(outs)
    shapes = tuple(
        pltpu.VMEM(out.shape, out.dtype) if spec is VMEM and i not in loose else out
        for i, (out, spec) in enumerate(zip(outs, specs))
    )
    run = pl.pallas_call(
        kernel,
        out_shape=shapes,
        in_specs=in_specs,
        out_specs=tuple(specs),
        scratch_shapes=list(scratch),
        compiler_params=pltpu.CompilerParams(vmem_limit_bytes=12 * 2**20),
        cost_estimate=pl.CostEstimate(flops=10**6, bytes_accessed=4 * 10**6, transcendentals=0),
    )

    def place(*args):
        placed = [
            arg if spec is SMEM else pltpu.with_memory_space_constraint(arg, spec.memory_space)
            for arg, spec in zip(args, in_specs)
        ]
        results = run(*placed)
        return results if many else results[0]

    return place


def exchange(x, axis):
    return lax.all_to_all(x, axis, split_axis=0, concat_axis=0, tiled=True)


def shift(x, groups, step):
    return lax.ppermute(x, "grp", [(g, (g + 2 * step) % groups) for g in range(groups)])


def swap(x, groups):
    return lax.ppermute(x, "grp", [(g, g ^ 1) for g in range(groups)])


def body(left, right, values, core, tile_slice, tile_fill):
    owners = lax.axis_size("own")
    groups = lax.axis_size("grp")
    chips = groups // 2
    tiles, rows, rank = left.shape
    per_device = core.shape[0]
    local_count = groups * per_device
    slots = 2 * owners
    packed_shape = (rank // 2, 2 * rank)
    along_x = [[2 * x + side for x in range(chips)] for side in range(2)]

    left_t = jnp.swapaxes(left, 1, 2)
    right_t = jnp.swapaxes(right, 1, 2)
    sds = jax.ShapeDtypeStruct
    slot_sds = sds((slots,) + packed_shape, BF16)
    mine_sds = sds((per_device,) + packed_shape, BF16)
    chip_shape = (chips, per_device) + packed_shape
    table_scr = pltpu.VMEM((local_count + 1,) + packed_shape, BF16)

    def exchange_x(x):
        return lax.all_to_all(
            x, "grp", split_axis=0, concat_axis=0, tiled=True, axis_index_groups=along_x
        )

    me = lax.axis_index("grp").astype(jnp.int32).reshape(1)

    slot, wanted, mine = call(
        functools.partial(prepare_kernel, owners, groups),
        [HBM, HBM],
        (sds((1, tiles), jnp.int32), sds((owners, 128), jnp.int32), mine_sds),
        [
            pltpu.VMEM(core.shape, BF16),
            pltpu.VMEM((1, tiles), jnp.int32),
            pltpu.SemaphoreType.DMA,
            pltpu.SemaphoreType.DMA,
        ],
    )(tile_slice.reshape(1, tiles), core)
    slot = slot.reshape(tiles)
    distant = {k: shift(mine, groups, -k) for k in range(2, chips, 2)}
    ids = exchange(wanted.reshape(owners, 1, 128), "own")
    adjacent = {k: shift(mine, groups, -k) for k in range(1, chips, 2)}
    pieces = [mine] + [{**distant, **adjacent}[k] for k in range(1, chips)]
    near = call(bundle_kernel, [VMEM] * chips, sds(chip_shape, BF16))(*pieces)
    outgoing = call(
        functools.partial(sided_kernel, True), [SMEM] * 2 + [VMEM] * 2, slot_sds, [table_scr]
    )(me, ids, near, swap(near, groups))
    got = exchange(outgoing, "own")
    grads = call(
        grad_kernel,
        [SMEM, SMEM, VMEM, VMEM, VMEM, VMEM],
        slot_sds,
        [pltpu.VMEM((tiles, rows), F32)],
    )(slot, tile_fill, left_t, right_t, values, got)
    got_grads = exchange(grads, "own")
    near, far = call(
        sum_kernel,
        [SMEM, VMEM, SMEM],
        (sds(chip_shape, F32), sds(chip_shape, BF16)),
        [pltpu.VMEM((local_count + 1,) + packed_shape, F32)],
    )(ids, got_grads, me)
    joined = call(join_kernel, [VMEM] * 2, sds(chip_shape, BF16))(near, swap(far, groups))
    new_spread, new_core = call(
        update_kernel, [VMEM] * 2, (sds(chip_shape, BF16), sds(core.shape, BF16)), loose=(1,)
    )(mine, exchange_x(joined))
    new_near = exchange_x(new_spread)
    new_far = swap(new_near, groups)
    outgoing = call(
        functools.partial(sided_kernel, False), [SMEM] * 2 + [VMEM] * 2, slot_sds, [table_scr])(
        me, ids, new_near, new_far
    )
    new_got = exchange(outgoing, "own")
    new_left_t = call(refresh_kernel, [SMEM, VMEM, VMEM], sds(left_t.shape, BF16), loose=(0,))(slot, left_t, new_got)
    return (new_core, jnp.swapaxes(new_left_t, 1, 2))


def solution(mesh):
    spec3 = P(("grp", "own"), None, None)
    spec2 = P(("grp", "own"), None)
    spec1 = P(("grp", "own"))
    return jax.shard_map(
        body,
        mesh=mesh,
        in_specs=(spec3, spec3, spec2, spec3, spec1, spec1),
        out_specs=(spec3, spec3),
        check_vma=False,
    )
```

```python
import functools

import jax
import jax.numpy as jnp
from jax import lax
from jax.experimental import pallas as pl
from jax.experimental.pallas import tpu as pltpu
from jax.sharding import PartitionSpec as P


VMEM = pl.BlockSpec(memory_space=pltpu.VMEM)
SMEM = pl.BlockSpec(memory_space=pltpu.SMEM)
HBM = pl.BlockSpec(memory_space=pltpu.HBM)
BF16 = jnp.bfloat16
F32 = jnp.float32
SHIFT = 16


def pack(square):
    half = square.shape[0] // 2
    return jnp.concatenate([square[:half], square[half:]], axis=1)


def unpack(packed):
    width = packed.shape[1] // 2
    return jnp.concatenate([packed[:, :width], packed[:, width:]], axis=0)


def prepare_kernel(
    owners, groups, tiles_ref, core_ref, slot_ref, wanted_ref, out_ref, core_scr, index_scr, sem, index_sem
):
    fetch_index = pltpu.make_async_copy(tiles_ref, index_scr, index_sem)
    fetch_index.start()
    fetch = pltpu.make_async_copy(core_ref, core_scr, sem)
    fetch.start()
    per_device = core_ref.shape[0]
    tiles = tiles_ref.shape[1]
    magic = -(-(2**SHIFT) // per_device)
    fetch_index.wait()
    index = index_scr[...]
    block = lax.shift_right_logical(index * magic, SHIFT)
    group = lax.shift_right_logical(block * -(-(2**SHIFT) // owners), SHIFT)
    owner = block - group * owners
    side_major = (group & 1) * (groups // 2) + lax.shift_right_logical(group, 1)
    local = (side_major - block) * per_device + index

    mine = jnp.broadcast_to(owner.astype(F32), (tiles, tiles))
    row = lax.broadcasted_iota(jnp.int32, (tiles, tiles), 0)
    col = lax.broadcasted_iota(jnp.int32, (tiles, tiles), 1)
    earlier = jnp.where((mine == mine.T) & (row < col), 1, 0)
    slot = 2 * owner + jnp.sum(earlier, axis=0, keepdims=True)
    slot_ref[...] = slot

    dead = groups * per_device
    lane = lax.broadcasted_iota(jnp.int32, wanted_ref.shape, 1)
    seat = 2 * lax.broadcasted_iota(jnp.int32, (owners, tiles), 0)
    asked = [
        jnp.sum(jnp.where(slot == seat + r, local - dead, 0), axis=1, keepdims=True) + dead
        for r in range(2)
    ]
    wanted_ref[...] = jnp.where(lane == 0, asked[0], asked[1])
    fetch.wait()
    for i in range(per_device):
        out_ref[i] = pack(core_scr[i].astype(F32).T).astype(BF16)


def pick_rows(ids_ref, table_ref, out_ref):
    table_ref[table_ref.shape[0] - 1] = jnp.zeros(table_ref.shape[1:], BF16)

    def step(k, carry):
        rows = [table_ref[ids_ref[4 * k + i // 2, 0, i % 2]] for i in range(8)]
        for i, row in enumerate(rows):
            out_ref[8 * k + i] = row
        return carry

    lax.fori_loop(0, out_ref.shape[0] // 8, step, 0, unroll=2)


def bundle_kernel(me_ref, *refs):
    pieces, out_ref = refs[:-1], refs[-1]
    for k, piece in enumerate(pieces):
        out_ref[lax.rem(lax.div(me_ref[0], 2) + k, len(pieces))] = piece[...]


def sided_kernel(me_ref, ids_ref, near_ref, far_ref, out_ref, table_ref):
    chips, size = near_ref.shape[:2]
    side = lax.rem(me_ref[0], 2)
    for x in range(chips):
        table_ref[pl.ds((side * chips + x) * size, size)] = near_ref[x]
        table_ref[pl.ds(((1 - side) * chips + x) * size, size)] = far_ref[x]
    pick_rows(ids_ref, table_ref, out_ref)


def grad_kernel(slot_ref, fill_ref, left_ref, right_ref, value_ref, slice_ref, out_ref, value_scr):
    value_scr[...] = value_ref[...].astype(F32)
    lanes = lax.broadcasted_iota(jnp.int32, (1, left_ref.shape[2]), 1)
    wide = left_ref.shape[0]

    def step(k, carry):
        tiles = [wide * k + i for i in range(wide)]
        slots = [slot_ref[t] for t in tiles]
        projected = [
            jnp.dot(unpack(slice_ref[slot]), left_ref[t], preferred_element_type=F32)
            for t, slot in zip(tiles, slots)
        ]
        grads = []
        for t, proj in zip(tiles, projected):
            predicted = jnp.sum(proj * right_ref[t].astype(F32), axis=0, keepdims=True)
            residual = jnp.where(
                lanes < fill_ref[t], predicted - value_scr[pl.ds(t, 1), :], 0.0
            )
            weighted = (residual * left_ref[t].astype(F32)).astype(BF16)
            grads.append(
                lax.dot_general(
                    right_ref[t],
                    weighted,
                    (((1,), (1,)), ((), ())),
                    preferred_element_type=F32,
                )
            )
        for slot, grad in zip(slots, grads):
            out_ref[slot] = pack(grad).astype(BF16)
        return carry

    lax.fori_loop(0, left_ref.shape[0] // wide, step, 0)


def add_side(side, ids_ref, grad_ref, acc_ref):
    size = acc_ref.shape[0] - 1
    acc_ref[...] = jnp.zeros_like(acc_ref)

    def step(c, carry):
        for r in range(2):
            row = ids_ref[c, 0, r] - side * size
            row = jnp.where((row >= 0) & (row < size), row, size)
            acc_ref[row] += grad_ref[2 * c + r].astype(F32)
        return carry

    lax.fori_loop(0, grad_ref.shape[0] // 2, step, 0, unroll=4)


def far_kernel(me_ref, ids_ref, grad_ref, out_ref, acc_ref):
    add_side(1 - lax.rem(me_ref[0], 2), ids_ref, grad_ref, acc_ref)
    size = out_ref.shape[1]
    for x in range(out_ref.shape[0]):
        out_ref[x] = acc_ref[x * size : (x + 1) * size].astype(BF16)


def near_kernel(me_ref, ids_ref, grad_ref, acc_ref):
    add_side(lax.rem(me_ref[0], 2), ids_ref, grad_ref, acc_ref)


def join_kernel(near_ref, other_ref, out_ref):
    size = out_ref.shape[1]
    for x in range(out_ref.shape[0]):
        near = near_ref[x * size : (x + 1) * size]
        out_ref[x] = (near + other_ref[x].astype(F32)).astype(BF16)


def update_kernel(table_ref, part_ref, packed_ref):
    total = jnp.sum(part_ref[...].astype(F32), axis=0)
    packed = (table_ref[...].astype(F32) - total).astype(BF16)
    for x in range(packed_ref.shape[0]):
        packed_ref[x] = packed


def core_kernel(packed_ref, out_ref):
    for i in range(out_ref.shape[0]):
        out_ref[i] = unpack(packed_ref[0, i].astype(F32)).T.astype(BF16)


def refresh_kernel(slot_ref, left_ref, slice_ref, out_ref):
    wide = left_ref.shape[0]

    def step(k, carry):
        tiles = [wide * k + i for i in range(wide)]
        fresh = [
            jnp.dot(unpack(slice_ref[slot_ref[t]]), left_ref[t], preferred_element_type=F32)
            for t in tiles
        ]
        for t, value in zip(tiles, fresh):
            out_ref[t] = value.astype(BF16)
        return carry

    lax.fori_loop(0, left_ref.shape[0] // wide, step, 0)


def call(kernel, in_specs, outs, scratch=(), out_specs=None, loose=()):
    many = isinstance(outs, tuple)
    outs = outs if many else (outs,)
    specs = out_specs or (VMEM,) * len(outs)
    shapes = tuple(
        pltpu.VMEM(out.shape, out.dtype) if spec is VMEM and i not in loose else out
        for i, (out, spec) in enumerate(zip(outs, specs))
    )
    run = pl.pallas_call(
        kernel,
        out_shape=shapes,
        in_specs=in_specs,
        out_specs=tuple(specs),
        scratch_shapes=list(scratch),
        compiler_params=pltpu.CompilerParams(vmem_limit_bytes=12 * 2**20),
        cost_estimate=pl.CostEstimate(flops=10**6, bytes_accessed=4 * 10**6, transcendentals=0),
    )

    def place(*args):
        placed = [
            arg if spec is SMEM else pltpu.with_memory_space_constraint(arg, spec.memory_space)
            for arg, spec in zip(args, in_specs)
        ]
        results = run(*placed)
        return results if many else results[0]

    return place


def exchange(x, axis):
    return lax.all_to_all(x, axis, split_axis=0, concat_axis=0, tiled=True)


def shift(x, groups, step):
    return lax.ppermute(x, "grp", [(g, (g + 2 * step) % groups) for g in range(groups)])


def swap(x, groups):
    return lax.ppermute(x, "grp", [(g, g ^ 1) for g in range(groups)])


def body(left, right, values, core, tile_slice, tile_fill):
    owners = lax.axis_size("own")
    groups = lax.axis_size("grp")
    chips = groups // 2
    tiles, rows, rank = left.shape
    per_device = core.shape[0]
    local_count = groups * per_device
    slots = 2 * owners
    packed_shape = (rank // 2, 2 * rank)
    along_x = [[2 * x + side for x in range(chips)] for side in range(2)]

    left_t = jnp.swapaxes(left, 1, 2)
    right_t = jnp.swapaxes(right, 1, 2)
    sds = jax.ShapeDtypeStruct
    slot_sds = sds((slots,) + packed_shape, BF16)
    mine_sds = sds((per_device,) + packed_shape, BF16)
    chip_shape = (chips, per_device) + packed_shape
    table_scr = pltpu.VMEM((local_count + 1,) + packed_shape, BF16)

    def exchange_x(x):
        return lax.all_to_all(
            x, "grp", split_axis=0, concat_axis=0, tiled=True, axis_index_groups=along_x
        )

    me = lax.axis_index("grp").astype(jnp.int32).reshape(1)

    slot, wanted, mine = call(
        functools.partial(prepare_kernel, owners, groups),
        [HBM, HBM],
        (sds((1, tiles), jnp.int32), sds((owners, 128), jnp.int32), mine_sds),
        [
            pltpu.VMEM(core.shape, BF16),
            pltpu.VMEM((1, tiles), jnp.int32),
            pltpu.SemaphoreType.DMA,
            pltpu.SemaphoreType.DMA,
        ],
    )(tile_slice.reshape(1, tiles), core)
    slot = slot.reshape(tiles)
    distant = {k: shift(mine, groups, -k) for k in range(2, chips, 2)}
    ids = exchange(wanted.reshape(owners, 1, 128), "own")
    adjacent = {k: shift(mine, groups, -k) for k in range(1, chips, 2)}
    pieces = [mine] + [{**distant, **adjacent}[k] for k in range(1, chips)]
    near = call(bundle_kernel, [SMEM] + [VMEM] * chips, sds(chip_shape, BF16))(me, *pieces)
    outgoing = call(
        sided_kernel, [SMEM] * 2 + [VMEM] * 2, slot_sds, [table_scr]
    )(me, ids, near, swap(near, groups))
    got = exchange(outgoing, "own")
    grads = call(
        grad_kernel,
        [SMEM, SMEM, VMEM, VMEM, VMEM, VMEM],
        slot_sds,
        [pltpu.VMEM((tiles, rows), F32)],
    )(slot, tile_fill, left_t, right_t, values, got)
    got_grads = exchange(grads, "own")
    side_rows = chips * per_device + 1
    far = call(
        far_kernel,
        [SMEM, SMEM, VMEM],
        sds(chip_shape, BF16),
        [pltpu.VMEM((side_rows,) + packed_shape, F32)],
    )(me, ids, got_grads)
    other = swap(far, groups)
    near = call(
        near_kernel, [SMEM, SMEM, VMEM], sds((side_rows,) + packed_shape, F32)
    )(me, ids, got_grads)
    joined = call(join_kernel, [VMEM] * 2, sds(chip_shape, BF16))(near, other)
    new_spread = call(update_kernel, [VMEM] * 2, sds(chip_shape, BF16))(mine, exchange_x(joined))
    new_near = exchange_x(new_spread)
    new_far = swap(new_near, groups)
    new_core = call(core_kernel, [VMEM], sds(core.shape, BF16), loose=(0,))(new_spread)
    outgoing = call(sided_kernel, [SMEM] * 2 + [VMEM] * 2, slot_sds, [table_scr])(
        me, ids, new_near, new_far
    )
    new_got = exchange(outgoing, "own")
    new_left_t = call(refresh_kernel, [SMEM, VMEM, VMEM], sds(left_t.shape, BF16), loose=(0,))(
        slot, left_t, new_got
    )
    return (new_core, jnp.swapaxes(new_left_t, 1, 2))


def solution(mesh):
    spec3 = P(("grp", "own"), None, None)
    spec2 = P(("grp", "own"), None)
    spec1 = P(("grp", "own"))
    return jax.shard_map(
        body,
        mesh=mesh,
        in_specs=(spec3, spec3, spec2, spec3, spec1, spec1),
        out_specs=(spec3, spec3),
        check_vma=False,
    )
```

```python
import functools

import jax
import jax.numpy as jnp
from jax import lax
from jax.experimental import pallas as pl
from jax.experimental.pallas import tpu as pltpu
from jax.sharding import PartitionSpec as P


VMEM = pl.BlockSpec(memory_space=pltpu.VMEM)
SMEM = pl.BlockSpec(memory_space=pltpu.SMEM)
HBM = pl.BlockSpec(memory_space=pltpu.HBM)
BF16 = jnp.bfloat16
F32 = jnp.float32
SHIFT = 16


def pack(square):
    half = square.shape[0] // 2
    return jnp.concatenate([square[:half], square[half:]], axis=1)


def unpack(packed):
    width = packed.shape[1] // 2
    return jnp.concatenate([packed[:, :width], packed[:, width:]], axis=0)


def prepare_kernel(
    owners, groups, tiles_ref, core_ref, slot_ref, wanted_ref, out_ref, core_scr, index_scr, sem, index_sem
):
    fetch_index = pltpu.make_async_copy(tiles_ref, index_scr, index_sem)
    fetch_index.start()
    fetch = pltpu.make_async_copy(core_ref, core_scr, sem)
    fetch.start()
    per_device = core_ref.shape[0]
    tiles = tiles_ref.shape[1]
    magic = -(-(2**SHIFT) // per_device)
    fetch_index.wait()
    index = index_scr[...]
    block = lax.shift_right_logical(index * magic, SHIFT)
    group = lax.shift_right_logical(block * -(-(2**SHIFT) // owners), SHIFT)
    owner = block - group * owners
    side_major = (group & 1) * (groups // 2) + lax.shift_right_logical(group, 1)
    local = (side_major - block) * per_device + index

    mine = jnp.broadcast_to(owner.astype(F32), (tiles, tiles))
    row = lax.broadcasted_iota(jnp.int32, (tiles, tiles), 0)
    col = lax.broadcasted_iota(jnp.int32, (tiles, tiles), 1)
    earlier = jnp.where((mine == mine.T) & (row < col), 1, 0)
    slot = 2 * owner + jnp.sum(earlier, axis=0, keepdims=True)
    slot_ref[...] = slot

    dead = groups * per_device
    lane = lax.broadcasted_iota(jnp.int32, wanted_ref.shape, 1)
    seat = 2 * lax.broadcasted_iota(jnp.int32, (owners, tiles), 0)
    asked = [
        jnp.sum(jnp.where(slot == seat + r, local - dead, 0), axis=1, keepdims=True) + dead
        for r in range(2)
    ]
    wanted_ref[...] = jnp.where(lane == 0, asked[0], asked[1])
    fetch.wait()
    for i in range(per_device):
        out_ref[i] = pack(core_scr[i].astype(F32).T).astype(BF16)


def pick_side(side, ids_ref, table_ref, out_ref, prior_ref=None):
    count = table_ref.shape[0]

    def step(k, carry):
        rows = []
        for i in range(8):
            row = ids_ref[4 * k + i // 2, 0, i % 2] - side * count
            inside = (row >= 0) & (row < count)
            value = table_ref[jnp.where(inside, row, 0)]
            if prior_ref is not None:
                value = jnp.where(inside, value, prior_ref[8 * k + i])
            rows.append(value)
        for i, value in enumerate(rows):
            out_ref[8 * k + i] = value
        return carry

    lax.fori_loop(0, out_ref.shape[0] // 8, step, 0, unroll=2)


def bundle_kernel(me_ref, *refs):
    pieces, out_ref = refs[:-1], refs[-1]
    for k, piece in enumerate(pieces):
        out_ref[lax.rem(lax.div(me_ref[0], 2) + k, len(pieces))] = piece[...]


def pick_near_kernel(me_ref, ids_ref, near_ref, out_ref):
    pick_side(lax.rem(me_ref[0], 2), ids_ref, near_ref, out_ref)


def pick_far_kernel(me_ref, ids_ref, far_ref, prior_ref, out_ref):
    pick_side(1 - lax.rem(me_ref[0], 2), ids_ref, far_ref, out_ref, prior_ref)


def grad_kernel(slot_ref, fill_ref, left_ref, right_ref, value_ref, slice_ref, out_ref, value_scr):
    value_scr[...] = value_ref[...].astype(F32)
    lanes = lax.broadcasted_iota(jnp.int32, (1, left_ref.shape[2]), 1)
    wide = left_ref.shape[0]

    def step(k, carry):
        tiles = [wide * k + i for i in range(wide)]
        slots = [slot_ref[t] for t in tiles]
        projected = [
            jnp.dot(unpack(slice_ref[slot]), left_ref[t], preferred_element_type=F32)
            for t, slot in zip(tiles, slots)
        ]
        grads = []
        for t, proj in zip(tiles, projected):
            predicted = jnp.sum(proj * right_ref[t].astype(F32), axis=0, keepdims=True)
            residual = jnp.where(
                lanes < fill_ref[t], predicted - value_scr[pl.ds(t, 1), :], 0.0
            )
            weighted = (residual * left_ref[t].astype(F32)).astype(BF16)
            grads.append(
                lax.dot_general(
                    right_ref[t],
                    weighted,
                    (((1,), (1,)), ((), ())),
                    preferred_element_type=F32,
                )
            )
        for slot, grad in zip(slots, grads):
            out_ref[slot] = pack(grad).astype(BF16)
        return carry

    lax.fori_loop(0, left_ref.shape[0] // wide, step, 0)


def add_side(side, ids_ref, grad_ref, acc_ref):
    size = acc_ref.shape[0] - 1
    acc_ref[...] = jnp.zeros_like(acc_ref)

    def step(c, carry):
        for r in range(2):
            row = ids_ref[c, 0, r] - side * size
            row = jnp.where((row >= 0) & (row < size), row, size)
            acc_ref[row] += grad_ref[2 * c + r].astype(F32)
        return carry

    lax.fori_loop(0, grad_ref.shape[0] // 2, step, 0, unroll=4)


def far_kernel(me_ref, ids_ref, grad_ref, out_ref, acc_ref):
    add_side(1 - lax.rem(me_ref[0], 2), ids_ref, grad_ref, acc_ref)
    size = out_ref.shape[1]
    for x in range(out_ref.shape[0]):
        out_ref[x] = acc_ref[x * size : (x + 1) * size].astype(BF16)


def near_kernel(me_ref, ids_ref, grad_ref, acc_ref):
    add_side(lax.rem(me_ref[0], 2), ids_ref, grad_ref, acc_ref)


def join_kernel(near_ref, other_ref, out_ref):
    size = out_ref.shape[1]
    for x in range(out_ref.shape[0]):
        near = near_ref[x * size : (x + 1) * size]
        out_ref[x] = (near + other_ref[x].astype(F32)).astype(BF16)


def update_kernel(table_ref, part_ref, packed_ref):
    total = jnp.sum(part_ref[...].astype(F32), axis=0)
    packed = (table_ref[...].astype(F32) - total).astype(BF16)
    for x in range(packed_ref.shape[0]):
        packed_ref[x] = packed


def core_kernel(packed_ref, out_ref):
    for i in range(out_ref.shape[0]):
        out_ref[i] = unpack(packed_ref[0, i].astype(F32)).T.astype(BF16)


def refresh_kernel(slot_ref, left_ref, slice_ref, out_ref):
    wide = left_ref.shape[0]

    def step(k, carry):
        tiles = [wide * k + i for i in range(wide)]
        fresh = [
            jnp.dot(unpack(slice_ref[slot_ref[t]]), left_ref[t], preferred_element_type=F32)
            for t in tiles
        ]
        for t, value in zip(tiles, fresh):
            out_ref[t] = value.astype(BF16)
        return carry

    lax.fori_loop(0, left_ref.shape[0] // wide, step, 0)


def call(kernel, in_specs, outs, scratch=(), out_specs=None, loose=()):
    many = isinstance(outs, tuple)
    outs = outs if many else (outs,)
    specs = out_specs or (VMEM,) * len(outs)
    shapes = tuple(
        pltpu.VMEM(out.shape, out.dtype) if spec is VMEM and i not in loose else out
        for i, (out, spec) in enumerate(zip(outs, specs))
    )
    run = pl.pallas_call(
        kernel,
        out_shape=shapes,
        in_specs=in_specs,
        out_specs=tuple(specs),
        scratch_shapes=list(scratch),
        compiler_params=pltpu.CompilerParams(vmem_limit_bytes=12 * 2**20),
        cost_estimate=pl.CostEstimate(flops=10**6, bytes_accessed=4 * 10**6, transcendentals=0),
    )

    def place(*args):
        placed = [
            arg if spec is SMEM else pltpu.with_memory_space_constraint(arg, spec.memory_space)
            for arg, spec in zip(args, in_specs)
        ]
        results = run(*placed)
        return results if many else results[0]

    return place


def exchange(x, axis):
    return lax.all_to_all(x, axis, split_axis=0, concat_axis=0, tiled=True)


def shift(x, groups, step):
    return lax.ppermute(x, "grp", [(g, (g + 2 * step) % groups) for g in range(groups)])


def swap(x, groups):
    return lax.ppermute(x, "grp", [(g, g ^ 1) for g in range(groups)])


def body(left, right, values, core, tile_slice, tile_fill):
    owners = lax.axis_size("own")
    groups = lax.axis_size("grp")
    chips = groups // 2
    tiles, rows, rank = left.shape
    per_device = core.shape[0]
    slots = 2 * owners
    packed_shape = (rank // 2, 2 * rank)
    along_x = [[2 * x + side for x in range(chips)] for side in range(2)]

    left_t = jnp.swapaxes(left, 1, 2)
    right_t = jnp.swapaxes(right, 1, 2)
    sds = jax.ShapeDtypeStruct
    slot_sds = sds((slots,) + packed_shape, BF16)
    mine_sds = sds((per_device,) + packed_shape, BF16)
    chip_shape = (chips, per_device) + packed_shape
    side_shape = (chips * per_device,) + packed_shape
    pick_near = call(pick_near_kernel, [SMEM] * 2 + [VMEM], slot_sds)
    pick_far = call(pick_far_kernel, [SMEM] * 2 + [VMEM] * 2, slot_sds)

    def exchange_x(x):
        return lax.all_to_all(
            x, "grp", split_axis=0, concat_axis=0, tiled=True, axis_index_groups=along_x
        )

    me = lax.axis_index("grp").astype(jnp.int32).reshape(1)

    slot, wanted, mine = call(
        functools.partial(prepare_kernel, owners, groups),
        [HBM, HBM],
        (sds((1, tiles), jnp.int32), sds((owners, 128), jnp.int32), mine_sds),
        [
            pltpu.VMEM(core.shape, BF16),
            pltpu.VMEM((1, tiles), jnp.int32),
            pltpu.SemaphoreType.DMA,
            pltpu.SemaphoreType.DMA,
        ],
    )(tile_slice.reshape(1, tiles), core)
    slot = slot.reshape(tiles)
    distant = {k: shift(mine, groups, -k) for k in range(2, chips, 2)}
    ids = exchange(wanted.reshape(owners, 1, 128), "own")
    adjacent = {k: shift(mine, groups, -k) for k in range(1, chips, 2)}
    pieces = [mine] + [{**distant, **adjacent}[k] for k in range(1, chips)]
    near = call(bundle_kernel, [SMEM] + [VMEM] * chips, sds(chip_shape, BF16))(me, *pieces)
    far = swap(near, groups)
    prior = pick_near(me, ids, near.reshape(side_shape))
    outgoing = pick_far(me, ids, far.reshape(side_shape), prior)
    got = exchange(outgoing, "own")
    grads = call(
        grad_kernel,
        [SMEM, SMEM, VMEM, VMEM, VMEM, VMEM],
        slot_sds,
        [pltpu.VMEM((tiles, rows), F32)],
    )(slot, tile_fill, left_t, right_t, values, got)
    got_grads = exchange(grads, "own")
    side_rows = chips * per_device + 1
    far = call(
        far_kernel,
        [SMEM, SMEM, VMEM],
        sds(chip_shape, BF16),
        [pltpu.VMEM((side_rows,) + packed_shape, F32)],
    )(me, ids, got_grads)
    other = swap(far, groups)
    near = call(
        near_kernel, [SMEM, SMEM, VMEM], sds((side_rows,) + packed_shape, F32)
    )(me, ids, got_grads)
    joined = call(join_kernel, [VMEM] * 2, sds(chip_shape, BF16))(near, other)
    new_spread = call(update_kernel, [VMEM] * 2, sds(chip_shape, BF16))(mine, exchange_x(joined))
    new_near = exchange_x(new_spread)
    new_far = swap(new_near, groups)
    new_core = call(core_kernel, [VMEM], sds(core.shape, BF16), loose=(0,))(new_spread)
    prior = pick_near(me, ids, new_near.reshape(side_shape))
    outgoing = pick_far(me, ids, new_far.reshape(side_shape), prior)
    new_got = exchange(outgoing, "own")
    new_left_t = call(refresh_kernel, [SMEM, VMEM, VMEM], sds(left_t.shape, BF16), loose=(0,))(
        slot, left_t, new_got
    )
    return (new_core, jnp.swapaxes(new_left_t, 1, 2))


def solution(mesh):
    spec3 = P(("grp", "own"), None, None)
    spec2 = P(("grp", "own"), None)
    spec1 = P(("grp", "own"))
    return jax.shard_map(
        body,
        mesh=mesh,
        in_specs=(spec3, spec3, spec2, spec3, spec1, spec1),
        out_specs=(spec3, spec3),
        check_vma=False,
    )
```

```python
import functools

import jax
import jax.numpy as jnp
from jax import lax
from jax.experimental import pallas as pl
from jax.experimental.pallas import tpu as pltpu
from jax.sharding import PartitionSpec as P


VMEM = pl.BlockSpec(memory_space=pltpu.VMEM)
SMEM = pl.BlockSpec(memory_space=pltpu.SMEM)
HBM = pl.BlockSpec(memory_space=pltpu.HBM)
BF16 = jnp.bfloat16
F32 = jnp.float32
SHIFT = 16


def pack(square):
    half = square.shape[0] // 2
    return jnp.concatenate([square[:half], square[half:]], axis=1)


def unpack(packed):
    width = packed.shape[1] // 2
    return jnp.concatenate([packed[:, :width], packed[:, width:]], axis=0)


def prepare_kernel(
    owners, groups, tiles_ref, core_ref, slot_ref, wanted_ref, out_ref, core_scr, index_scr, sem, index_sem
):
    fetch_index = pltpu.make_async_copy(tiles_ref, index_scr, index_sem)
    fetch_index.start()
    fetch = pltpu.make_async_copy(core_ref, core_scr, sem)
    fetch.start()
    per_device = core_ref.shape[0]
    tiles = tiles_ref.shape[1]
    magic = -(-(2**SHIFT) // per_device)
    fetch_index.wait()
    index = index_scr[...]
    block = lax.shift_right_logical(index * magic, SHIFT)
    group = lax.shift_right_logical(block * -(-(2**SHIFT) // owners), SHIFT)
    owner = block - group * owners
    side_major = (group & 1) * (groups // 2) + lax.shift_right_logical(group, 1)
    local = (side_major - block) * per_device + index

    mine = jnp.broadcast_to(owner.astype(F32), (tiles, tiles))
    row = lax.broadcasted_iota(jnp.int32, (tiles, tiles), 0)
    col = lax.broadcasted_iota(jnp.int32, (tiles, tiles), 1)
    earlier = jnp.where((mine == mine.T) & (row < col), 1, 0)
    slot = 2 * owner + jnp.sum(earlier, axis=0, keepdims=True)
    slot_ref[...] = slot

    dead = groups * per_device
    lane = lax.broadcasted_iota(jnp.int32, wanted_ref.shape, 1)
    seat = 2 * lax.broadcasted_iota(jnp.int32, (owners, tiles), 0)
    asked = [
        jnp.sum(jnp.where(slot == seat + r, local - dead, 0), axis=1, keepdims=True) + dead
        for r in range(2)
    ]
    wanted_ref[...] = jnp.where(lane == 0, asked[0], asked[1])
    fetch.wait()
    for i in range(per_device):
        out_ref[i] = pack(core_scr[i].astype(F32).T).astype(BF16)


def pick_rows(ids_ref, table_ref, out_ref):
    table_ref[table_ref.shape[0] - 1] = jnp.zeros(table_ref.shape[1:], BF16)

    def step(k, carry):
        rows = [table_ref[ids_ref[8 * k + i]] for i in range(8)]
        for i, row in enumerate(rows):
            out_ref[8 * k + i] = row
        return carry

    lax.fori_loop(0, out_ref.shape[0] // 8, step, 0, unroll=2)


def compact_kernel(ids_ref, out_ref):
    for c in range(ids_ref.shape[0]):
        for r in range(2):
            out_ref[2 * c + r] = ids_ref[c, 0, r]


def bundle_kernel(me_ref, *refs):
    pieces, out_ref = refs[:-1], refs[-1]
    for k, piece in enumerate(pieces):
        out_ref[lax.rem(lax.div(me_ref[0], 2) + k, len(pieces))] = piece[...]


def sided_kernel(me_ref, ids_ref, near_ref, far_ref, out_ref, table_ref):
    chips, size = near_ref.shape[:2]
    side = lax.rem(me_ref[0], 2)
    for x in range(chips):
        table_ref[pl.ds((side * chips + x) * size, size)] = near_ref[x]
        table_ref[pl.ds(((1 - side) * chips + x) * size, size)] = far_ref[x]
    pick_rows(ids_ref, table_ref, out_ref)


def grad_kernel(slot_ref, fill_ref, left_ref, right_ref, value_ref, slice_ref, out_ref, value_scr):
    value_scr[...] = value_ref[...].astype(F32)
    lanes = lax.broadcasted_iota(jnp.int32, (1, left_ref.shape[2]), 1)
    wide = left_ref.shape[0]

    def step(k, carry):
        tiles = [wide * k + i for i in range(wide)]
        slots = [slot_ref[t] for t in tiles]
        projected = [
            jnp.dot(unpack(slice_ref[slot]), left_ref[t], preferred_element_type=F32)
            for t, slot in zip(tiles, slots)
        ]
        grads = []
        for t, proj in zip(tiles, projected):
            predicted = jnp.sum(proj * right_ref[t].astype(F32), axis=0, keepdims=True)
            residual = jnp.where(
                lanes < fill_ref[t], predicted - value_scr[pl.ds(t, 1), :], 0.0
            )
            weighted = (residual * left_ref[t].astype(F32)).astype(BF16)
            grads.append(
                lax.dot_general(
                    right_ref[t],
                    weighted,
                    (((1,), (1,)), ((), ())),
                    preferred_element_type=F32,
                )
            )
        for slot, grad in zip(slots, grads):
            out_ref[slot] = pack(grad).astype(BF16)
        return carry

    lax.fori_loop(0, left_ref.shape[0] // wide, step, 0)


def add_side(side, ids_ref, grad_ref, acc_ref):
    size = acc_ref.shape[0] - 1
    acc_ref[...] = jnp.zeros_like(acc_ref)

    def step(c, carry):
        for r in range(2):
            row = ids_ref[2 * c + r] - side * size
            row = jnp.where((row >= 0) & (row < size), row, size)
            acc_ref[row] += grad_ref[2 * c + r].astype(F32)
        return carry

    lax.fori_loop(0, grad_ref.shape[0] // 2, step, 0, unroll=4)


def far_kernel(me_ref, ids_ref, grad_ref, out_ref, acc_ref):
    add_side(1 - lax.rem(me_ref[0], 2), ids_ref, grad_ref, acc_ref)
    size = out_ref.shape[1]
    for x in range(out_ref.shape[0]):
        out_ref[x] = acc_ref[x * size : (x + 1) * size].astype(BF16)


def near_kernel(me_ref, ids_ref, grad_ref, acc_ref):
    add_side(lax.rem(me_ref[0], 2), ids_ref, grad_ref, acc_ref)


def join_kernel(near_ref, other_ref, out_ref):
    size = out_ref.shape[1]
    for x in range(out_ref.shape[0]):
        near = near_ref[x * size : (x + 1) * size]
        out_ref[x] = (near + other_ref[x].astype(F32)).astype(BF16)


def update_kernel(table_ref, part_ref, packed_ref):
    total = jnp.sum(part_ref[...].astype(F32), axis=0)
    packed = (table_ref[...].astype(F32) - total).astype(BF16)
    for x in range(packed_ref.shape[0]):
        packed_ref[x] = packed


def core_kernel(packed_ref, out_ref):
    for i in range(out_ref.shape[0]):
        out_ref[i] = unpack(packed_ref[0, i].astype(F32)).T.astype(BF16)


def refresh_kernel(slot_ref, left_ref, slice_ref, out_ref):
    wide = left_ref.shape[0]

    def step(k, carry):
        tiles = [wide * k + i for i in range(wide)]
        fresh = [
            jnp.dot(unpack(slice_ref[slot_ref[t]]), left_ref[t], preferred_element_type=F32)
            for t in tiles
        ]
        for t, value in zip(tiles, fresh):
            out_ref[t] = value.astype(BF16)
        return carry

    lax.fori_loop(0, left_ref.shape[0] // wide, step, 0)


def call(kernel, in_specs, outs, scratch=(), out_specs=None, loose=()):
    many = isinstance(outs, tuple)
    outs = outs if many else (outs,)
    specs = out_specs or (VMEM,) * len(outs)
    shapes = tuple(
        pltpu.VMEM(out.shape, out.dtype) if spec is VMEM and i not in loose else out
        for i, (out, spec) in enumerate(zip(outs, specs))
    )
    run = pl.pallas_call(
        kernel,
        out_shape=shapes,
        in_specs=in_specs,
        out_specs=tuple(specs),
        scratch_shapes=list(scratch),
        compiler_params=pltpu.CompilerParams(vmem_limit_bytes=12 * 2**20),
        cost_estimate=pl.CostEstimate(flops=10**6, bytes_accessed=4 * 10**6, transcendentals=0),
    )

    def place(*args):
        placed = [
            arg if spec is SMEM else pltpu.with_memory_space_constraint(arg, spec.memory_space)
            for arg, spec in zip(args, in_specs)
        ]
        results = run(*placed)
        return results if many else results[0]

    return place


def exchange(x, axis):
    return lax.all_to_all(x, axis, split_axis=0, concat_axis=0, tiled=True)


def shift(x, groups, step):
    return lax.ppermute(x, "grp", [(g, (g + 2 * step) % groups) for g in range(groups)])


def swap(x, groups):
    return lax.ppermute(x, "grp", [(g, g ^ 1) for g in range(groups)])


def body(left, right, values, core, tile_slice, tile_fill):
    owners = lax.axis_size("own")
    groups = lax.axis_size("grp")
    chips = groups // 2
    tiles, rows, rank = left.shape
    per_device = core.shape[0]
    local_count = groups * per_device
    slots = 2 * owners
    packed_shape = (rank // 2, 2 * rank)
    along_x = [[2 * x + side for x in range(chips)] for side in range(2)]

    left_t = jnp.swapaxes(left, 1, 2)
    right_t = jnp.swapaxes(right, 1, 2)
    sds = jax.ShapeDtypeStruct
    slot_sds = sds((slots,) + packed_shape, BF16)
    mine_sds = sds((per_device,) + packed_shape, BF16)
    chip_shape = (chips, per_device) + packed_shape
    table_scr = pltpu.VMEM((local_count + 1,) + packed_shape, BF16)

    def exchange_x(x):
        return lax.all_to_all(
            x, "grp", split_axis=0, concat_axis=0, tiled=True, axis_index_groups=along_x
        )

    me = lax.axis_index("grp").astype(jnp.int32).reshape(1)

    slot, wanted, mine = call(
        functools.partial(prepare_kernel, owners, groups),
        [HBM, HBM],
        (sds((1, tiles), jnp.int32), sds((owners, 128), jnp.int32), mine_sds),
        [
            pltpu.VMEM(core.shape, BF16),
            pltpu.VMEM((1, tiles), jnp.int32),
            pltpu.SemaphoreType.DMA,
            pltpu.SemaphoreType.DMA,
        ],
    )(tile_slice.reshape(1, tiles), core)
    slot = slot.reshape(tiles)
    distant = {k: shift(mine, groups, -k) for k in range(2, chips, 2)}
    ids = exchange(wanted.reshape(owners, 1, 128), "own")
    adjacent = {k: shift(mine, groups, -k) for k in range(1, chips, 2)}
    pieces = [mine] + [{**distant, **adjacent}[k] for k in range(1, chips)]
    near = call(bundle_kernel, [SMEM] + [VMEM] * chips, sds(chip_shape, BF16))(me, *pieces)
    far = swap(near, groups)
    ids = call(compact_kernel, [SMEM], sds((slots,), jnp.int32), out_specs=(SMEM,))(ids)
    outgoing = call(sided_kernel, [SMEM] * 2 + [VMEM] * 2, slot_sds, [table_scr])(
        me, ids, near, far
    )
    got = exchange(outgoing, "own")
    grads = call(
        grad_kernel,
        [SMEM, SMEM, VMEM, VMEM, VMEM, VMEM],
        slot_sds,
        [pltpu.VMEM((tiles, rows), F32)],
    )(slot, tile_fill, left_t, right_t, values, got)
    got_grads = exchange(grads, "own")
    side_rows = chips * per_device + 1
    far = call(
        far_kernel,
        [SMEM, SMEM, VMEM],
        sds(chip_shape, BF16),
        [pltpu.VMEM((side_rows,) + packed_shape, F32)],
    )(me, ids, got_grads)
    other = swap(far, groups)
    near = call(
        near_kernel, [SMEM, SMEM, VMEM], sds((side_rows,) + packed_shape, F32)
    )(me, ids, got_grads)
    joined = call(join_kernel, [VMEM] * 2, sds(chip_shape, BF16))(near, other)
    new_spread = call(update_kernel, [VMEM] * 2, sds(chip_shape, BF16))(mine, exchange_x(joined))
    new_near = exchange_x(new_spread)
    new_far = swap(new_near, groups)
    new_core = call(core_kernel, [VMEM], sds(core.shape, BF16), loose=(0,))(new_spread)
    outgoing = call(sided_kernel, [SMEM] * 2 + [VMEM] * 2, slot_sds, [table_scr])(
        me, ids, new_near, new_far
    )
    new_got = exchange(outgoing, "own")
    new_left_t = call(refresh_kernel, [SMEM, VMEM, VMEM], sds(left_t.shape, BF16), loose=(0,))(
        slot, left_t, new_got
    )
    return (new_core, jnp.swapaxes(new_left_t, 1, 2))


def solution(mesh):
    spec3 = P(("grp", "own"), None, None)
    spec2 = P(("grp", "own"), None)
    spec1 = P(("grp", "own"))
    return jax.shard_map(
        body,
        mesh=mesh,
        in_specs=(spec3, spec3, spec2, spec3, spec1, spec1),
        out_specs=(spec3, spec3),
        check_vma=False,
    )
```
